512 devices in a mesh: ctx: 16 (over z), ch: 32 (over x, y, core).
Axes of the slice: x: 4, y: 4, z: 16, core: 2. Of those that a mesh axis runs over, the one named last changes fastest.
Arguments:
- features: bfloat16 [2, 16, 128, 3, 4096], P(None, 'ctx', None, None, 'ch'), may hold values from -6 to 6
- short_weight: bfloat16 [7, 3, 4096], P(None, None, 'ch'), may hold values from -2 to 2
- long_filter: bfloat16 [2, 16, 128, 4096], P(None, 'ctx', None, 'ch'), may hold values from -0.125 to 0.125
- skip_gain: float32 [4096], P('ch'), may hold values from -4 to 4
- out_weight: bfloat16 [4096, 4096], P('ch'), may hold values from -0.1875 to 0.1875
Outputs:
- mixed: bfloat16 [2, 16, 128, 4096], P(None, 'ctx', None, 'ch')
The draws below stay inside these ranges and needn't reach their ends.
All inputs are finite; a program needn't handle non-finite values.
Results may differ from the reference program's by a relative error of at most 0.015.
Values may be sent and summed in bfloat16 or wider, within the bound.
No kernel may reach another device: no remote copies, remote signals or barrier semaphores. Data moves between devices by JAX's collectives and lax.ppermute only.
A program may use at most 64 MiB of HBM per device.

```python
import jax
import jax.numpy as jnp

D = 4096
BLOCK = 128
TAPS = 7
PAIRS = 16
SEQ = 4096


def strengthened(values, key, source, target, blocks, factor):
    def block_of(position):
        return (jnp.arange(values.shape[position]) // (values.shape[position] // blocks)).reshape((-1,) + (1,) * (values.ndim - 1 - position))

    first = jax.random.permutation(key, blocks)[block_of(target)]
    other_side = (block_of(target) + blocks // 2) % blocks
    return jnp.where((block_of(source) == first) | (block_of(source) == other_side), factor * values, values)


def block_levels(own_key, extent, split, low, high):
    def one(dim, parts):
        heights = jax.random.uniform(jax.random.fold_in(jax.random.fold_in(own_key, 6), dim), (parts,), jnp.float32, low / len(split), high / len(split))
        return jnp.repeat(jnp.exp(heights), extent[dim] // parts).reshape((-1,) + (1,) * (len(extent) - dim - 1))

    factor_of = one(*split[0])
    for cut in split[1:]:
        factor_of = factor_of * one(*cut)
    return factor_of


def gaussian(stream_key, shape, width, bound, shards=(), held_as=jnp.bfloat16):
    entries = width * jax.random.normal(stream_key, shape, jnp.float32)
    if shards:
        entries = entries * block_levels(stream_key, shape, shards, -0.22, 0.18)
    return jnp.clip(entries, -bound, bound).astype(held_as)


def bell_draw_with(key, extent, deviation, most, shards, heavy, kind=jnp.bfloat16):
    result = deviation * jax.random.normal(key, extent, jnp.float32)
    if shards:
        result = result * block_levels(key, extent, shards, -0.22, 0.18)
    return jnp.clip(strengthened(result, jax.random.fold_in(key, 3), *heavy), -most, most).astype(kind)


def setup_inputs(seed: int = 0) -> dict:
    seeds = jax.random.split(jax.random.key(seed), 6)
    return {
        "features": gaussian(seeds[0], (2, PAIRS, BLOCK, 3, D), 1.0, 6.0, ((1, 16), (4, 32))),
        "short_weight": gaussian(seeds[1], (TAPS, 3, D), TAPS ** -0.5, 2.0, ((2, 32),)),
        "long_filter": gaussian(seeds[2], (2, PAIRS, BLOCK, D), (SEQ // 2) ** -0.5, 0.125, ((1, 16), (3, 32))),
        "skip_gain": gaussian(seeds[3], (D,), 1.0, 4.0, ((0, 32),), jnp.float32),
        "out_weight": bell_draw_with(seeds[4], (D, D), D ** -0.5, 0.1875, ((0, 32),), (0, 1, 32, 2.75)),
    }


def ordered(blocks):
    return jnp.concatenate([blocks[0], jnp.flip(blocks[1], axis=0)], axis=0)


def reference(features, short_weight, long_filter, skip_gain, out_weight):
    sequence = ordered(features).reshape((SEQ, 3, D)).astype(jnp.float32)
    margin_rows = TAPS - 1
    padded = jnp.pad(sequence, ((margin_rows, 0), (0, 0), (0, 0)))
    kernel = short_weight.astype(jnp.float32)
    featured = jnp.zeros_like(sequence)
    for offset in range(TAPS):
        featured = featured + kernel[offset] * padded[margin_rows - offset: margin_rows - offset + SEQ]
    queries = featured[:, 0]
    gated_keys = (featured[:, 1] * featured[:, 2]).astype(jnp.bfloat16)
    signal = gated_keys.astype(jnp.float32)
    response = ordered(long_filter).reshape((SEQ, D)).astype(jnp.float32)
    product = jnp.fft.rfft(signal, n=2 * SEQ, axis=0) * jnp.fft.rfft(response, n=2 * SEQ, axis=0)
    convolved = jnp.fft.irfft(product, n=2 * SEQ, axis=0)[:SEQ]
    activated = (queries * (convolved + skip_gain.astype(jnp.float32) * signal)).astype(jnp.bfloat16)
    mixed = jnp.dot(activated, out_weight, preferred_element_type=jnp.float32).astype(jnp.bfloat16)
    blocks = mixed.reshape((2 * PAIRS, BLOCK, D))
    return jnp.stack([blocks[:PAIRS], jnp.flip(blocks[PAIRS:], axis=0)], axis=0)
```

```python
import math

import jax
import jax.numpy as jnp
import numpy as np
from jax import lax
from jax.experimental import pallas as pl
from jax.experimental.pallas import tpu as pltpu
from jax.sharding import Mesh, PartitionSpec as P

INTERPRET = False
LANES = 128
PERIOD = 2 * LANES


def tables():
    t = np.arange(LANES)[:, None]
    k = np.arange(LANES)[None, :]
    angle = 2.0 * math.pi * ((t * k) % PERIOD) / PERIOD
    sign = np.where(t % 2 == 0, 1.0, -1.0)
    cosine, sine = np.cos(angle), -np.sin(angle)
    forward = np.concatenate([cosine, np.where(k == 0, sign, sine)], axis=1)
    scale = np.where(k == 0, 1.0, 2.0) / PERIOD
    inverse = np.concatenate(
        [cosine * scale, np.where(k == 0, sign / PERIOD, sine * scale)], axis=1
    ).T
    high = forward.astype(jnp.bfloat16)
    low = (forward - high.astype(np.float64)).astype(jnp.bfloat16)
    return np.stack([high, low]), inverse.astype(np.float32)


def pack_kernel(index_ref, features_ref, filter_ref, taps_ref, gain_ref, out_ref, weights_ref, rows, turned):
    groups = out_ref.shape[0]
    channels = LANES // groups
    streams = features_ref.shape[1]
    for half in range(2):
        for stream in range(streams):
            tile = features_ref[half, stream].astype(jnp.float32).T.astype(jnp.bfloat16)
            out_ref[:, half * streams + stream] = tile.reshape(groups, channels, LANES)
        tile = filter_ref[half].astype(jnp.float32).T.astype(jnp.bfloat16)
        out_ref[:, 2 * streams + half] = tile.reshape(groups, channels, LANES)
    rows[...] = jnp.zeros_like(rows)
    taps = taps_ref.shape[1]
    for stream in range(streams):
        rows[stream * 8 : stream * 8 + taps] = taps_ref[stream].astype(jnp.float32)
    rows[streams * 8 : streams * 8 + 1] = gain_ref[...]
    turned[...] = rows[...].T
    first = pl.multiple_of(index_ref[0] * channels, channels)
    weights_ref[...] = turned[pl.ds(first, channels)]


def mix_kernel(packed_ref, weights_ref, forward_ref, inverse_ref, out_ref, query, keys, lags, key_spec, lag_spec, resp, total):
    pairs = packed_ref.shape[0]
    blocks = 2 * pairs
    channels = packed_ref.shape[2]
    taps = 7
    lane = lax.broadcasted_iota(jnp.int32, (channels, LANES), 1)

    def place(block):
        return (block, 0) if block < pairs else (blocks - 1 - block, 1)

    def span(block):
        return slice(block * channels, (block + 1) * channels)

    def column(index):
        return jnp.broadcast_to(weights_ref[:, index : index + 1], (channels, LANES))

    for block in range(blocks):
        source, half = place(block)
        lags[span(block)] = packed_ref[source, 6 + half]
    for stream in (1, 2, 0):
        weight = [column(stream * 8 + i) for i in range(taps)]
        turned_before = [jnp.zeros((channels, LANES), jnp.float32)] * taps
        for block in range(blocks):
            source, half = place(block)
            value = packed_ref[source, half * 3 + stream].astype(jnp.float32)
            summed = weight[0] * value
            turned = [value]
            for i in range(1, taps):
                rolled = pltpu.roll(value, i, 1)
                turned.append(rolled)
                summed = summed + weight[i] * jnp.where(lane >= i, rolled, turned_before[i])
            turned_before = turned
            if stream == 1:
                total[span(block), :LANES] = summed
            elif stream == 2:
                keys[span(block)] = (total[span(block), :LANES] * summed).astype(jnp.bfloat16)
            else:
                query[span(block)] = summed

    def transform(values):
        return jnp.dot(values, forward_ref[0], preferred_element_type=jnp.float32) + jnp.dot(
            values, forward_ref[1], preferred_element_type=jnp.float32
        )

    key_spec[...] = transform(keys[...])
    lag_spec[...] = transform(lags[...])
    parity = jnp.where(lane % 2 == 0, 1.0, -1.0).astype(jnp.float32)
    for block in range(blocks):
        real = lag_spec[span(block), :LANES]
        imag = lag_spec[span(block), LANES:]
        if block:
            real = real + parity * lag_spec[span(block - 1), :LANES]
            imag = imag + parity * lag_spec[span(block - 1), LANES:]
        resp[0, span(block)] = real
        resp[1, span(block)] = jnp.where(lane == 0, 0.0, imag)
        resp[2, span(block)] = jnp.where(lane == 0, imag, real)
    group = 4
    for base in range(0, blocks, group):
        sums = [[None, None] for _ in range(group)]
        for block in range(base + group):
            real = key_spec[span(block), :LANES]
            imag = key_spec[span(block), LANES:]
            for j in range(group):
                gap = base + j - block
                if gap < 0:
                    continue
                first = resp[0, span(gap)]
                cross = resp[1, span(gap)]
                second = resp[2, span(gap)]
                out_real = real * first - imag * cross
                out_imag = real * cross + imag * second
                if sums[j][0] is None:
                    sums[j] = [out_real, out_imag]
                else:
                    sums[j] = [sums[j][0] + out_real, sums[j][1] + out_imag]
        for j in range(group):
            total[span(base + j), :LANES] = sums[j][0]
            total[span(base + j), LANES:] = sums[j][1]
    convolved = jnp.dot(
        total[...], inverse_ref[...], preferred_element_type=jnp.float32, precision=lax.Precision.HIGHEST
    )
    total[:, :LANES] = convolved
    gain = column(24)
    for block in range(blocks):
        target, half = place(block)
        inner = total[span(block), :LANES] + gain * keys[span(block)].astype(jnp.float32)
        out_ref[target, half] = (query[span(block)] * inner).astype(jnp.bfloat16)


def project_kernel(index_ref, own_ref, other_ref, own_weight_ref, other_weight_ref, out_ref):
    chips, rows, width = out_ref.shape
    depth = own_weight_ref.shape[0]
    core = index_ref[0]
    lhs = []
    for half in range(2):
        parts = [
            ref[:, half].reshape(depth, LANES).astype(jnp.float32).T.astype(jnp.bfloat16)
            for ref in (own_ref, other_ref)
        ]
        lhs.append(jnp.concatenate(parts, axis=1))
    lhs = jnp.concatenate(lhs, axis=0)
    for chip in range(chips):
        columns = pl.ds(pl.multiple_of((2 * chip + core) * width, width), width)
        weight = jnp.concatenate([own_weight_ref[:, columns], other_weight_ref[:, columns]], axis=0)
        out_ref[chip] = jnp.dot(lhs, weight, preferred_element_type=jnp.float32).astype(jnp.bfloat16)


def local(features, short_weight, long_filter, skip_gain, out_weight):
    pairs = lax.axis_size("ctx")
    chips = lax.axis_size("chip")
    length = features.shape[2]
    width = features.shape[4]
    channels = width // pairs
    position = lax.axis_index("ctx").astype(jnp.int32).reshape(1)
    core = lax.axis_index("core").astype(jnp.int32).reshape(1)
    other_weight = lax.ppermute(out_weight, "core", [(0, 1), (1, 0)])
    tiles = jnp.transpose(features, (0, 1, 3, 2, 4)).reshape(2, 3, length, width)
    taps = jnp.transpose(short_weight, (1, 0, 2))
    scalars = pl.BlockSpec(memory_space=pltpu.SMEM)
    vmem = pl.BlockSpec(memory_space=pltpu.VMEM)
    packed, weights = pl.pallas_call(
        pack_kernel,
        out_shape=(
            jax.ShapeDtypeStruct((pairs, 8, channels, length), jnp.bfloat16),
            jax.ShapeDtypeStruct((channels, LANES), jnp.float32),
        ),
        in_specs=[scalars] + [vmem] * 4,
        out_specs=(vmem, vmem),
        scratch_shapes=[pltpu.VMEM((LANES, LANES), jnp.float32)] * 2,
        cost_estimate=pl.CostEstimate(flops=1000000, bytes_accessed=600000, transcendentals=0),
        interpret=INTERPRET,
    )(position, tiles, long_filter.reshape(2, length, width), taps, skip_gain.reshape(1, width))
    packed = lax.all_to_all(packed, "ctx", 0, 0, tiled=True)
    forward, inverse = tables()
    rows = 2 * pairs * channels
    activated = pl.pallas_call(
        mix_kernel,
        out_shape=jax.ShapeDtypeStruct((pairs, 2, channels, length), jnp.bfloat16),
        in_specs=[vmem] * 4,
        out_specs=vmem,
        scratch_shapes=[
            pltpu.VMEM((rows, LANES), jnp.float32),
            pltpu.VMEM((rows, LANES), jnp.bfloat16),
            pltpu.VMEM((rows, LANES), jnp.bfloat16),
            pltpu.VMEM((rows, PERIOD), jnp.float32),
            pltpu.VMEM((rows, PERIOD), jnp.float32),
            pltpu.VMEM((3, rows, LANES), jnp.float32),
            pltpu.VMEM((rows, PERIOD), jnp.float32),
        ],
        cost_estimate=pl.CostEstimate(flops=100000000, bytes_accessed=600000, transcendentals=0),
        interpret=INTERPRET,
    )(packed, weights, jnp.asarray(forward), jnp.asarray(inverse))
    own = lax.all_to_all(activated, "ctx", 0, 0, tiled=True)
    other = lax.ppermute(own, "core", [(0, 1), (1, 0)])
    partial = pl.pallas_call(
        project_kernel,
        out_shape=jax.ShapeDtypeStruct((chips, 2 * length, width), jnp.bfloat16),
        in_specs=[scalars] + [vmem] * 4,
        out_specs=vmem,
        cost_estimate=pl.CostEstimate(flops=268435456, bytes_accessed=3300000, transcendentals=0),
        interpret=INTERPRET,
    )(core, own, other, out_weight, other_weight)
    shares = lax.all_to_all(partial, "chip", 0, 0, tiled=True)
    mixed = jnp.sum(shares.astype(jnp.float32), axis=0).astype(jnp.bfloat16)
    return mixed.reshape(2, 1, length, width)


def solution(mesh):
    pairs, parts = mesh.shape["ctx"], mesh.shape["ch"]
    split = Mesh(mesh.devices.reshape(pairs, parts // 2, 2), ("ctx", "chip", "core"))
    ch = ("chip", "core")
    in_specs = (
        P(None, "ctx", None, None, ch),
        P(None, None, ch),
        P(None, "ctx", None, ch),
        P(ch),
        P(ch, None),
    )
    return jax.shard_map(
        local, mesh=split, in_specs=in_specs, out_specs=P(None, "ctx", None, ch), check_vma=False
    )
```

```python
import math

import jax
import jax.numpy as jnp
import numpy as np
from jax import lax
from jax.experimental import pallas as pl
from jax.experimental.pallas import tpu as pltpu
from jax.sharding import Mesh, PartitionSpec as P

INTERPRET = False
MIB = 2**20
LANES = 128
PERIOD = 2 * LANES


def in_hbm(value):
    return pltpu.with_memory_space_constraint(value, pltpu.HBM)


def tables():
    t = np.arange(LANES)[:, None]
    k = np.arange(LANES)[None, :]
    angle = 2.0 * math.pi * ((t * k) % PERIOD) / PERIOD
    sign = np.where(t % 2 == 0, 1.0, -1.0)
    cosine, sine = np.cos(angle), -np.sin(angle)
    forward = np.concatenate([cosine, np.where(k == 0, sign, sine)], axis=1)
    scale = np.where(k == 0, 1.0, 2.0) / PERIOD
    inverse = np.concatenate(
        [cosine * scale, np.where(k == 0, sign / PERIOD, sine * scale)], axis=1
    ).T
    high = forward.astype(jnp.bfloat16)
    low = (forward - high.astype(np.float64)).astype(jnp.bfloat16)
    return np.stack([high, low]), inverse.astype(np.float32)


def pack_kernel(
    index_ref, features_hbm, filter_hbm, taps_hbm, gain_hbm, out_ref, weights_ref,
    features_ref, filter_ref, taps_ref, gain_ref, rows, turned, sems,
):
    groups = out_ref.shape[0]
    channels = LANES // groups
    streams = features_ref.shape[1]
    copies = [
        pltpu.make_async_copy(features_hbm.at[0], features_ref.at[0], sems.at[0]),
        pltpu.make_async_copy(features_hbm.at[1], features_ref.at[1], sems.at[1]),
        pltpu.make_async_copy(filter_hbm, filter_ref, sems.at[2]),
        pltpu.make_async_copy(taps_hbm, taps_ref, sems.at[3]),
        pltpu.make_async_copy(gain_hbm, gain_ref, sems.at[4]),
    ]
    for copy in copies:
        copy.start()
    for half in range(2):
        copies[half].wait()
        for stream in range(streams):
            tile = features_ref[half, stream].astype(jnp.float32).T.astype(jnp.bfloat16)
            out_ref[:, half * streams + stream] = tile.reshape(groups, channels, LANES)
    copies[2].wait()
    for half in range(2):
        tile = filter_ref[half].astype(jnp.float32).T.astype(jnp.bfloat16)
        out_ref[:, 2 * streams + half] = tile.reshape(groups, channels, LANES)
    rows[...] = jnp.zeros_like(rows)
    taps = taps_ref.shape[1]
    copies[3].wait()
    copies[4].wait()
    for stream in range(streams):
        rows[stream * 8 : stream * 8 + taps] = taps_ref[stream].astype(jnp.float32)
    rows[streams * 8 : streams * 8 + 1] = gain_ref[...]
    turned[...] = rows[...].T
    first = pl.multiple_of(index_ref[0] * channels, channels)
    weights_ref[...] = turned[pl.ds(first, channels)]


def mix_kernel(
    packed_ref, weights_ref, forward_hbm, inverse_hbm, out_ref,
    query, keys, lags, key_spec, lag_spec, resp, total, forward_ref, inverse_ref, sems,
):
    forward_copy = pltpu.make_async_copy(forward_hbm, forward_ref, sems.at[0])
    inverse_copy = pltpu.make_async_copy(inverse_hbm, inverse_ref, sems.at[1])
    forward_copy.start()
    inverse_copy.start()
    pairs = packed_ref.shape[0]
    blocks = 2 * pairs
    channels = packed_ref.shape[2]
    taps = 7
    lane = lax.broadcasted_iota(jnp.int32, (channels, LANES), 1)

    def place(block):
        return (block, 0) if block < pairs else (blocks - 1 - block, 1)

    def span(block):
        return slice(block * channels, (block + 1) * channels)

    def column(index):
        return jnp.broadcast_to(weights_ref[:, index : index + 1], (channels, LANES))

    for block in range(blocks):
        source, half = place(block)
        lags[span(block)] = packed_ref[source, 6 + half]
    for stream in (1, 2, 0):
        weight = [column(stream * 8 + i) for i in range(taps)]
        turned_before = [jnp.zeros((channels, LANES), jnp.float32)] * taps
        for block in range(blocks):
            source, half = place(block)
            value = packed_ref[source, half * 3 + stream].astype(jnp.float32)
            summed = weight[0] * value
            turned = [value]
            for i in range(1, taps):
                rolled = pltpu.roll(value, i, 1)
                turned.append(rolled)
                summed = summed + weight[i] * jnp.where(lane >= i, rolled, turned_before[i])
            turned_before = turned
            if stream == 1:
                total[span(block), :LANES] = summed
            elif stream == 2:
                keys[span(block)] = (total[span(block), :LANES] * summed).astype(jnp.bfloat16)
            else:
                query[span(block)] = summed

    def transform(values):
        return jnp.dot(values, forward_ref[0], preferred_element_type=jnp.float32) + jnp.dot(
            values, forward_ref[1], preferred_element_type=jnp.float32
        )

    forward_copy.wait()
    key_spec[...] = transform(keys[...])
    lag_spec[...] = transform(lags[...])
    parity = jnp.where(lane % 2 == 0, 1.0, -1.0).astype(jnp.float32)
    for block in range(blocks):
        real = lag_spec[span(block), :LANES]
        imag = lag_spec[span(block), LANES:]
        if block:
            real = real + parity * lag_spec[span(block - 1), :LANES]
            imag = imag + parity * lag_spec[span(block - 1), LANES:]
        resp[0, span(block)] = real
        resp[1, span(block)] = jnp.where(lane == 0, 0.0, imag)
        resp[2, span(block)] = jnp.where(lane == 0, imag, real)
    group = 4
    for base in range(0, blocks, group):
        sums = [[None, None] for _ in range(group)]
        for block in range(base + group):
            real = key_spec[span(block), :LANES]
            imag = key_spec[span(block), LANES:]
            for j in range(group):
                gap = base + j - block
                if gap < 0:
                    continue
                first = resp[0, span(gap)]
                cross = resp[1, span(gap)]
                second = resp[2, span(gap)]
                out_real = real * first - imag * cross
                out_imag = real * cross + imag * second
                if sums[j][0] is None:
                    sums[j] = [out_real, out_imag]
                else:
                    sums[j] = [sums[j][0] + out_real, sums[j][1] + out_imag]
        for j in range(group):
            total[span(base + j), :LANES] = sums[j][0]
            total[span(base + j), LANES:] = sums[j][1]
    inverse_copy.wait()
    convolved = jnp.dot(
        total[...], inverse_ref[...], preferred_element_type=jnp.float32, precision=lax.Precision.HIGHEST
    )
    total[:, :LANES] = convolved
    gain = column(24)
    for block in range(blocks):
        target, half = place(block)
        inner = total[span(block), :LANES] + gain * keys[span(block)].astype(jnp.float32)
        out_ref[target, half] = (query[span(block)] * inner).astype(jnp.bfloat16)


def project_kernel(index_ref, own_ref, other_ref, own_weight_ref, other_weight_ref, out_ref):
    chips, rows, width = out_ref.shape
    depth = own_weight_ref.shape[0]
    core = index_ref[0]
    lhs = []
    for half in range(2):
        parts = [
            ref[:, half].reshape(depth, LANES).astype(jnp.float32).T.astype(jnp.bfloat16)
            for ref in (own_ref, other_ref)
        ]
        lhs.append(jnp.concatenate(parts, axis=1))
    lhs = jnp.concatenate(lhs, axis=0)
    for chip in range(chips):
        columns = pl.ds(pl.multiple_of((2 * chip + core) * width, width), width)
        weight = jnp.concatenate([own_weight_ref[:, columns], other_weight_ref[:, columns]], axis=0)
        out_ref[chip] = jnp.dot(lhs, weight, preferred_element_type=jnp.float32).astype(jnp.bfloat16)


def local(features, short_weight, long_filter, skip_gain, out_weight):
    pairs = lax.axis_size("ctx")
    chips = lax.axis_size("chip")
    length = features.shape[2]
    width = features.shape[4]
    channels = width // pairs
    position = lax.axis_index("ctx").astype(jnp.int32).reshape(1)
    core = lax.axis_index("core").astype(jnp.int32).reshape(1)
    other_weight = lax.ppermute(out_weight, "core", [(0, 1), (1, 0)])
    tiles = jnp.transpose(features, (0, 1, 3, 2, 4)).reshape(2, 3, length, width)
    taps = jnp.transpose(short_weight, (1, 0, 2))
    scalars = pl.BlockSpec(memory_space=pltpu.SMEM)
    vmem = pl.BlockSpec(memory_space=pltpu.VMEM)
    hbm = pl.BlockSpec(memory_space=pltpu.HBM)
    packed, weights = pl.pallas_call(
        pack_kernel,
        out_shape=(
            pltpu.VMEM((pairs, 8, channels, length), jnp.bfloat16),
            pltpu.VMEM((channels, LANES), jnp.float32),
        ),
        in_specs=[scalars] + [hbm] * 4,
        out_specs=(vmem, vmem),
        scratch_shapes=[
            pltpu.VMEM((2, 3, length, width), jnp.bfloat16),
            pltpu.VMEM((2, length, width), jnp.bfloat16),
            pltpu.VMEM(taps.shape, jnp.bfloat16),
            pltpu.VMEM((1, width), jnp.float32),
            pltpu.VMEM((LANES, LANES), jnp.float32),
            pltpu.VMEM((LANES, LANES), jnp.float32),
            pltpu.SemaphoreType.DMA((5,)),
        ],
        compiler_params=pltpu.CompilerParams(vmem_limit_bytes=4 * MIB),
        cost_estimate=pl.CostEstimate(flops=1000000, bytes_accessed=600000, transcendentals=0),
        interpret=INTERPRET,
    )(
        position,
        in_hbm(tiles),
        in_hbm(long_filter.reshape(2, length, width)),
        in_hbm(taps),
        in_hbm(skip_gain.reshape(1, width)),
    )
    packed = lax.all_to_all(packed, "ctx", 0, 0, tiled=True)
    forward, inverse = tables()
    rows = 2 * pairs * channels
    activated = pl.pallas_call(
        mix_kernel,
        out_shape=pltpu.VMEM((pairs, 2, channels, length), jnp.bfloat16),
        in_specs=[vmem] * 2 + [hbm] * 2,
        out_specs=vmem,
        scratch_shapes=[
            pltpu.VMEM((rows, LANES), jnp.float32),
            pltpu.VMEM((rows, LANES), jnp.bfloat16),
            pltpu.VMEM((rows, LANES), jnp.bfloat16),
            pltpu.VMEM((rows, PERIOD), jnp.float32),
            pltpu.VMEM((rows, PERIOD), jnp.float32),
            pltpu.VMEM((3, rows, LANES), jnp.float32),
            pltpu.VMEM((rows, PERIOD), jnp.float32),
            pltpu.VMEM(forward.shape, jnp.bfloat16),
            pltpu.VMEM(inverse.shape, jnp.float32),
            pltpu.SemaphoreType.DMA((2,)),
        ],
        compiler_params=pltpu.CompilerParams(vmem_limit_bytes=6 * MIB),
        cost_estimate=pl.CostEstimate(flops=100000000, bytes_accessed=600000, transcendentals=0),
        interpret=INTERPRET,
    )(
        packed,
        weights,
        in_hbm(jnp.asarray(forward)),
        in_hbm(jnp.asarray(inverse)),
    )
    own = lax.all_to_all(activated, "ctx", 0, 0, tiled=True)
    other = lax.ppermute(own, "core", [(0, 1), (1, 0)])
    partial = pl.pallas_call(
        project_kernel,
        out_shape=pltpu.VMEM((chips, 2 * length, width), jnp.bfloat16),
        in_specs=[scalars] + [vmem] * 4,
        out_specs=vmem,
        compiler_params=pltpu.CompilerParams(vmem_limit_bytes=8 * MIB),
        cost_estimate=pl.CostEstimate(flops=268435456, bytes_accessed=3300000, transcendentals=0),
        interpret=INTERPRET,
    )(core, own, other, out_weight, other_weight)
    shares = lax.all_to_all(partial, "chip", 0, 0, tiled=True)
    mixed = jnp.sum(shares.astype(jnp.float32), axis=0).astype(jnp.bfloat16)
    return mixed.reshape(2, 1, length, width)


def solution(mesh):
    pairs, parts = mesh.shape["ctx"], mesh.shape["ch"]
    split = Mesh(mesh.devices.reshape(pairs, parts // 2, 2), ("ctx", "chip", "core"))
    ch = ("chip", "core")
    in_specs = (
        P(None, "ctx", None, None, ch),
        P(None, None, ch),
        P(None, "ctx", None, ch),
        P(ch),
        P(ch, None),
    )
    return jax.shard_map(
        local, mesh=split, in_specs=in_specs, out_specs=P(None, "ctx", None, ch), check_vma=False
    )
```

```python
import math

import jax
import jax.numpy as jnp
import numpy as np
from jax import lax
from jax.experimental import pallas as pl
from jax.experimental.pallas import tpu as pltpu
from jax.sharding import Mesh, PartitionSpec as P

INTERPRET = False
MIB = 2**20
LANES = 128
PERIOD = 2 * LANES


def in_hbm(value):
    return pltpu.with_memory_space_constraint(value, pltpu.HBM)


def tables():
    t = np.arange(LANES)[:, None]
    k = np.arange(LANES)[None, :]
    angle = 2.0 * math.pi * ((t * k) % PERIOD) / PERIOD
    sign = np.where(t % 2 == 0, 1.0, -1.0)
    cosine, sine = np.cos(angle), -np.sin(angle)
    forward = np.concatenate([cosine, np.where(k == 0, sign, sine)], axis=1)
    scale = np.where(k == 0, 1.0, 2.0) / PERIOD
    inverse = np.concatenate(
        [cosine * scale, np.where(k == 0, sign / PERIOD, sine * scale)], axis=1
    ).T
    high = forward.astype(jnp.bfloat16)
    low = (forward - high.astype(np.float64)).astype(jnp.bfloat16)
    return np.stack([high, low]), inverse.astype(np.float32)


def pack_kernel(
    index_ref, features_hbm, filter_hbm, taps_hbm, gain_hbm, out_ref, weights_ref,
    features_ref, filter_ref, taps_ref, gain_ref, rows, turned, sems,
):
    groups = out_ref.shape[0]
    channels = LANES // groups
    streams = features_ref.shape[1]
    copies = [
        pltpu.make_async_copy(features_hbm.at[0], features_ref.at[0], sems.at[0]),
        pltpu.make_async_copy(features_hbm.at[1], features_ref.at[1], sems.at[1]),
        pltpu.make_async_copy(filter_hbm, filter_ref, sems.at[2]),
        pltpu.make_async_copy(taps_hbm, taps_ref, sems.at[3]),
        pltpu.make_async_copy(gain_hbm, gain_ref, sems.at[4]),
    ]
    for copy in copies:
        copy.start()
    for half in range(2):
        copies[half].wait()
        for stream in range(streams):
            tile = features_ref[half, stream].astype(jnp.float32).T.astype(jnp.bfloat16)
            out_ref[:, half * streams + stream] = tile.reshape(groups, channels, LANES)
    copies[2].wait()
    for half in range(2):
        tile = filter_ref[half].astype(jnp.float32).T.astype(jnp.bfloat16)
        out_ref[:, 2 * streams + half] = tile.reshape(groups, channels, LANES)
    rows[...] = jnp.zeros_like(rows)
    taps = taps_ref.shape[1]
    copies[3].wait()
    copies[4].wait()
    for stream in range(streams):
        rows[stream * 8 : stream * 8 + taps] = taps_ref[stream].astype(jnp.float32)
    rows[streams * 8 : streams * 8 + 1] = gain_ref[...]
    turned[...] = rows[...].T
    first = pl.multiple_of(index_ref[0] * channels, channels)
    weights_ref[...] = turned[pl.ds(first, channels)]


def mix_kernel(
    packed_ref, weights_ref, forward_hbm, inverse_hbm, out_ref,
    query, keys, lags, key_spec, lag_spec, resp, total, forward_ref, inverse_ref, sems,
):
    forward_copy = pltpu.make_async_copy(forward_hbm, forward_ref, sems.at[0])
    inverse_copy = pltpu.make_async_copy(inverse_hbm, inverse_ref, sems.at[1])
    forward_copy.start()
    inverse_copy.start()
    pairs = packed_ref.shape[0]
    blocks = 2 * pairs
    channels = packed_ref.shape[2]
    taps = 7
    lane = lax.broadcasted_iota(jnp.int32, (channels, LANES), 1)

    def place(block):
        owner, half = (block, 0) if block < pairs else (blocks - 1 - block, 1)
        return (owner + pairs // 2) % pairs, half

    def span(block):
        return slice(block * channels, (block + 1) * channels)

    def column(index):
        return jnp.broadcast_to(weights_ref[:, index : index + 1], (channels, LANES))

    for block in range(blocks):
        source, half = place(block)
        lags[span(block)] = packed_ref[source, 6 + half]
    for stream in (1, 2, 0):
        weight = [column(stream * 8 + i) for i in range(taps)]
        turned_before = [jnp.zeros((channels, LANES), jnp.float32)] * taps
        for block in range(blocks):
            source, half = place(block)
            value = packed_ref[source, half * 3 + stream].astype(jnp.float32)
            summed = weight[0] * value
            turned = [value]
            for i in range(1, taps):
                rolled = pltpu.roll(value, i, 1)
                turned.append(rolled)
                summed = summed + weight[i] * jnp.where(lane >= i, rolled, turned_before[i])
            turned_before = turned
            if stream == 1:
                total[span(block), :LANES] = summed
            elif stream == 2:
                keys[span(block)] = (total[span(block), :LANES] * summed).astype(jnp.bfloat16)
            else:
                query[span(block)] = summed

    def transform(values):
        return jnp.dot(values, forward_ref[0], preferred_element_type=jnp.float32) + jnp.dot(
            values, forward_ref[1], preferred_element_type=jnp.float32
        )

    forward_copy.wait()
    key_spec[...] = transform(keys[...])
    lag_spec[...] = transform(lags[...])
    parity = jnp.where(lane % 2 == 0, 1.0, -1.0).astype(jnp.float32)
    for block in range(blocks):
        real = lag_spec[span(block), :LANES]
        imag = lag_spec[span(block), LANES:]
        if block:
            real = real + parity * lag_spec[span(block - 1), :LANES]
            imag = imag + parity * lag_spec[span(block - 1), LANES:]
        resp[0, span(block)] = real
        resp[1, span(block)] = jnp.where(lane == 0, 0.0, imag)
        resp[2, span(block)] = jnp.where(lane == 0, imag, real)
    group = 4
    for base in range(0, blocks, group):
        sums = [[None, None] for _ in range(group)]
        for block in range(base + group):
            real = key_spec[span(block), :LANES]
            imag = key_spec[span(block), LANES:]
            for j in range(group):
                gap = base + j - block
                if gap < 0:
                    continue
                first = resp[0, span(gap)]
                cross = resp[1, span(gap)]
                second = resp[2, span(gap)]
                out_real = real * first - imag * cross
                out_imag = real * cross + imag * second
                if sums[j][0] is None:
                    sums[j] = [out_real, out_imag]
                else:
                    sums[j] = [sums[j][0] + out_real, sums[j][1] + out_imag]
        for j in range(group):
            total[span(base + j), :LANES] = sums[j][0]
            total[span(base + j), LANES:] = sums[j][1]
    inverse_copy.wait()
    convolved = jnp.dot(
        total[...], inverse_ref[...], preferred_element_type=jnp.float32, precision=lax.Precision.HIGHEST
    )
    total[:, :LANES] = convolved
    gain = column(24)
    for block in range(blocks):
        target, half = place(block)
        inner = total[span(block), :LANES] + gain * keys[span(block)].astype(jnp.float32)
        out_ref[target, half] = (query[span(block)] * inner).astype(jnp.bfloat16)


def project_kernel(index_ref, both_ref, own_weight_ref, other_weight_ref, out_ref):
    chips, rows, width = out_ref.shape
    depth = own_weight_ref.shape[0]
    core = index_ref[0]
    lhs = []
    for half in range(2):
        parts = [
            both_ref[which, :, half].reshape(depth, LANES).astype(jnp.float32).T.astype(jnp.bfloat16)
            for which in (core, 1 - core)
        ]
        lhs.append(jnp.concatenate(parts, axis=1))
    lhs = jnp.concatenate(lhs, axis=0)
    for chip in range(chips):
        columns = pl.ds(pl.multiple_of((2 * chip + core) * width, width), width)
        weight = jnp.concatenate([own_weight_ref[:, columns], other_weight_ref[:, columns]], axis=0)
        out_ref[chip] = jnp.dot(lhs, weight, preferred_element_type=jnp.float32).astype(jnp.bfloat16)


def local(features, short_weight, long_filter, skip_gain, out_weight):
    pairs = lax.axis_size("ctx")
    chips = lax.axis_size("chip")
    length = features.shape[2]
    width = features.shape[4]
    channels = width // pairs
    order = [[(place + pairs // 2) % pairs for place in range(pairs)]]
    position = ((lax.axis_index("ctx") + pairs // 2) % pairs).astype(jnp.int32).reshape(1)
    core = lax.axis_index("core").astype(jnp.int32).reshape(1)
    other_weight = lax.ppermute(out_weight, "core", [(0, 1), (1, 0)])
    tiles = jnp.transpose(features, (0, 1, 3, 2, 4)).reshape(2, 3, length, width)
    taps = jnp.transpose(short_weight, (1, 0, 2))
    scalars = pl.BlockSpec(memory_space=pltpu.SMEM)
    vmem = pl.BlockSpec(memory_space=pltpu.VMEM)
    hbm = pl.BlockSpec(memory_space=pltpu.HBM)
    packed, weights = pl.pallas_call(
        pack_kernel,
        out_shape=(
            pltpu.VMEM((pairs, 8, channels, length), jnp.bfloat16),
            pltpu.VMEM((channels, LANES), jnp.float32),
        ),
        in_specs=[scalars] + [hbm] * 4,
        out_specs=(vmem, vmem),
        scratch_shapes=[
            pltpu.VMEM((2, 3, length, width), jnp.bfloat16),
            pltpu.VMEM((2, length, width), jnp.bfloat16),
            pltpu.VMEM(taps.shape, jnp.bfloat16),
            pltpu.VMEM((1, width), jnp.float32),
            pltpu.VMEM((LANES, LANES), jnp.float32),
            pltpu.VMEM((LANES, LANES), jnp.float32),
            pltpu.SemaphoreType.DMA((5,)),
        ],
        compiler_params=pltpu.CompilerParams(vmem_limit_bytes=4 * MIB),
        cost_estimate=pl.CostEstimate(flops=1000000, bytes_accessed=600000, transcendentals=0),
        interpret=INTERPRET,
    )(
        position,
        in_hbm(tiles),
        in_hbm(long_filter.reshape(2, length, width)),
        in_hbm(taps),
        in_hbm(skip_gain.reshape(1, width)),
    )
    packed = lax.all_to_all(packed, "ctx", 0, 0, tiled=True, axis_index_groups=order)
    forward, inverse = tables()
    rows = 2 * pairs * channels
    activated = pl.pallas_call(
        mix_kernel,
        out_shape=pltpu.VMEM((pairs, 2, channels, length), jnp.bfloat16),
        in_specs=[vmem] * 2 + [hbm] * 2,
        out_specs=vmem,
        scratch_shapes=[
            pltpu.VMEM((rows, LANES), jnp.float32),
            pltpu.VMEM((rows, LANES), jnp.bfloat16),
            pltpu.VMEM((rows, LANES), jnp.bfloat16),
            pltpu.VMEM((rows, PERIOD), jnp.float32),
            pltpu.VMEM((rows, PERIOD), jnp.float32),
            pltpu.VMEM((3, rows, LANES), jnp.float32),
            pltpu.VMEM((rows, PERIOD), jnp.float32),
            pltpu.VMEM(forward.shape, jnp.bfloat16),
            pltpu.VMEM(inverse.shape, jnp.float32),
            pltpu.SemaphoreType.DMA((2,)),
        ],
        compiler_params=pltpu.CompilerParams(vmem_limit_bytes=6 * MIB),
        cost_estimate=pl.CostEstimate(flops=100000000, bytes_accessed=600000, transcendentals=0),
        interpret=INTERPRET,
    )(
        packed,
        weights,
        in_hbm(jnp.asarray(forward)),
        in_hbm(jnp.asarray(inverse)),
    )
    own = lax.all_to_all(activated, "ctx", 0, 0, tiled=True, axis_index_groups=order)
    both = lax.all_gather(own, "core", axis=0)
    partial = pl.pallas_call(
        project_kernel,
        out_shape=pltpu.VMEM((chips, 2 * length, width), jnp.bfloat16),
        in_specs=[scalars] + [vmem] * 3,
        out_specs=vmem,
        compiler_params=pltpu.CompilerParams(vmem_limit_bytes=8 * MIB),
        cost_estimate=pl.CostEstimate(flops=268435456, bytes_accessed=3300000, transcendentals=0),
        interpret=INTERPRET,
    )(core, both, out_weight, other_weight)
    shares = lax.all_to_all(partial, "chip", 0, 0, tiled=True)
    mixed = jnp.sum(shares.astype(jnp.float32), axis=0).astype(jnp.bfloat16)
    return mixed.reshape(2, 1, length, width)


def solution(mesh):
    pairs, parts = mesh.shape["ctx"], mesh.shape["ch"]
    split = Mesh(mesh.devices.reshape(pairs, parts // 2, 2), ("ctx", "chip", "core"))
    ch = ("chip", "core")
    in_specs = (
        P(None, "ctx", None, None, ch),
        P(None, None, ch),
        P(None, "ctx", None, ch),
        P(ch),
        P(ch, None),
    )
    return jax.shard_map(
        local, mesh=split, in_specs=in_specs, out_specs=P(None, "ctx", None, ch), check_vma=False
    )
```

```python
import math

import jax
import jax.numpy as jnp
import numpy as np
from jax import lax
from jax.experimental import pallas as pl
from jax.experimental.pallas import tpu as pltpu
from jax.sharding import Mesh, PartitionSpec as P

INTERPRET = False
MIB = 2**20
LANES = 128
PERIOD = 2 * LANES


def in_hbm(value):
    return pltpu.with_memory_space_constraint(value, pltpu.HBM)


def tables():
    t = np.arange(LANES)[:, None]
    k = np.arange(LANES)[None, :]
    angle = 2.0 * math.pi * ((t * k) % PERIOD) / PERIOD
    sign = np.where(t % 2 == 0, 1.0, -1.0)
    cosine, sine = np.cos(angle), -np.sin(angle)
    forward = np.concatenate([cosine, np.where(k == 0, sign, sine)], axis=1)
    scale = np.where(k == 0, 1.0, 2.0) / PERIOD
    inverse = np.concatenate(
        [cosine * scale, np.where(k == 0, sign / PERIOD, sine * scale)], axis=1
    ).T
    high = forward.astype(jnp.bfloat16)
    low = (forward - high.astype(np.float64)).astype(jnp.bfloat16)
    return np.stack([high, low]), inverse.astype(np.float32)


def pack_kernel(
    index_ref, features_hbm, filter_hbm, taps_hbm, gain_hbm, out_ref, weights_ref, query_ref,
    features_ref, filter_ref, taps_ref, gain_ref, extended, edges, rows, turned, sems,
):
    groups = out_ref.shape[0]
    channels = LANES // groups
    streams = features_ref.shape[1]
    taps = taps_ref.shape[1]
    rim = taps - 1
    copies = [
        pltpu.make_async_copy(taps_hbm, taps_ref, sems.at[3]),
        pltpu.make_async_copy(features_hbm.at[0], features_ref.at[0], sems.at[0]),
        pltpu.make_async_copy(features_hbm.at[1], features_ref.at[1], sems.at[1]),
        pltpu.make_async_copy(filter_hbm, filter_ref, sems.at[2]),
        pltpu.make_async_copy(gain_hbm, gain_ref, sems.at[4]),
    ]
    for copy in copies:
        copy.start()

    def put(row, tile):
        out_ref[:, row] = tile.T.astype(jnp.bfloat16).reshape(groups, channels, LANES)

    extended[:, :8] = jnp.zeros((streams, 8, LANES), jnp.float32)
    edges[...] = jnp.zeros_like(edges)
    rows[...] = jnp.zeros_like(rows)
    copies[0].wait()
    for half in range(2):
        copies[1 + half].wait()
        featured = []
        for stream in range(streams):
            value = features_ref[half, stream].astype(jnp.float32)
            extended[stream, 8:] = value
            base = 2 * rim * (half * streams + stream)
            edges[base : base + rim] = extended[stream, 8 + LANES - rim : 8 + LANES]
            edges[base + rim : base + 2 * rim] = extended[stream, 8 : 8 + rim]
            summed = taps_ref[stream, 0:1].astype(jnp.float32) * value
            for i in range(1, taps):
                weight = taps_ref[stream, i : i + 1].astype(jnp.float32)
                summed = summed + weight * extended[stream, 8 - i : 8 - i + LANES]
            featured.append(summed)
        query_ref[half] = featured[0]
        put(half, featured[1] * featured[2])
    copies[3].wait()
    for half in range(2):
        put(2 + half, filter_ref[half].astype(jnp.float32))
    put(4, edges[...])
    copies[4].wait()
    for stream in range(streams):
        rows[stream * 8 : stream * 8 + taps] = taps_ref[stream].astype(jnp.float32)
    rows[streams * 8 : streams * 8 + 1] = gain_ref[...]
    turned[...] = rows[...].T
    first = pl.multiple_of(index_ref[0] * channels, channels)
    weights_ref[...] = turned[pl.ds(first, channels)]


def mix_kernel(
    packed_ref, weights_ref, forward_hbm, inverse_hbm, out_ref,
    query, keys, lags, key_spec, lag_spec, resp, total, forward_ref, inverse_ref, sems,
):
    forward_copy = pltpu.make_async_copy(forward_hbm, forward_ref, sems.at[0])
    inverse_copy = pltpu.make_async_copy(inverse_hbm, inverse_ref, sems.at[1])
    forward_copy.start()
    inverse_copy.start()
    pairs = packed_ref.shape[0]
    blocks = 2 * pairs
    channels = packed_ref.shape[2]
    streams, taps = 3, 7
    rim = taps - 1
    step = 2 * rim
    lane = lax.broadcasted_iota(jnp.int32, (channels, LANES), 1)

    def place(block):
        owner, half = (block, 0) if block < pairs else (blocks - 1 - block, 1)
        return (owner + pairs // 2) % pairs, half

    def span(block):
        return slice(block * channels, (block + 1) * channels)

    def column(index):
        return jnp.broadcast_to(weights_ref[:, index : index + 1], (channels, LANES))

    for block in range(blocks):
        source, half = place(block)
        lags[span(block)] = packed_ref[source, 2 + half]
    stream_of = lane // step % streams
    weight = [
        jnp.where(stream_of == 0, column(i), jnp.where(stream_of == 1, column(8 + i), column(16 + i)))
        for i in range(taps)
    ]
    tail = lane % step < rim
    lower = lane < streams * step
    edge = [packed_ref[place(owner)[0], 4].astype(jnp.float32) for owner in range(pairs)]
    head = lane < rim
    for owner in range(pairs):
        before = edge[owner - 1] if owner else jnp.zeros_like(edge[0])
        if owner + 1 < pairs:
            after = edge[owner + 1]
        else:
            after = pltpu.roll(edge[owner], streams * step, 1)
        value = jnp.where(tail, jnp.where(lower, before, after), edge[owner])
        summed = weight[0] * value
        for i in range(1, taps):
            summed = summed + weight[i] * pltpu.roll(value, i, 1)
        product = summed * pltpu.roll(summed, LANES - step, 1)
        for half, block in ((0, owner), (1, blocks - 1 - owner)):
            first = half * streams * step + rim
            gated = pltpu.roll(product, LANES - first - step, 1)
            whole = packed_ref[place(owner)[0], half].astype(jnp.float32)
            keys[span(block)] = jnp.where(head, gated, whole).astype(jnp.bfloat16)
            query[span(block)] = pltpu.roll(summed, LANES - first, 1)

    def transform(values):
        return jnp.dot(values, forward_ref[0], preferred_element_type=jnp.float32) + jnp.dot(
            values, forward_ref[1], preferred_element_type=jnp.float32
        )

    forward_copy.wait()
    key_spec[...] = transform(keys[...])
    lag_spec[...] = transform(lags[...])
    parity = jnp.where(lane % 2 == 0, 1.0, -1.0).astype(jnp.float32)
    for block in range(blocks):
        real = lag_spec[span(block), :LANES]
        imag = lag_spec[span(block), LANES:]
        if block:
            real = real + parity * lag_spec[span(block - 1), :LANES]
            imag = imag + parity * lag_spec[span(block - 1), LANES:]
        resp[0, span(block)] = real
        resp[1, span(block)] = jnp.where(lane == 0, 0.0, imag)
        resp[2, span(block)] = jnp.where(lane == 0, imag, real)
    group = 4
    for base in range(0, blocks, group):
        sums = [[None, None] for _ in range(group)]
        for block in range(base + group):
            real = key_spec[span(block), :LANES]
            imag = key_spec[span(block), LANES:]
            for j in range(group):
                gap = base + j - block
                if gap < 0:
                    continue
                first = resp[0, span(gap)]
                cross = resp[1, span(gap)]
                second = resp[2, span(gap)]
                out_real = real * first - imag * cross
                out_imag = real * cross + imag * second
                if sums[j][0] is None:
                    sums[j] = [out_real, out_imag]
                else:
                    sums[j] = [sums[j][0] + out_real, sums[j][1] + out_imag]
        for j in range(group):
            total[span(base + j), :LANES] = sums[j][0]
            total[span(base + j), LANES:] = sums[j][1]
    inverse_copy.wait()
    convolved = jnp.dot(
        total[...], inverse_ref[...], preferred_element_type=jnp.float32, precision=lax.Precision.HIGHEST
    )
    total[:, :LANES] = convolved
    gain = column(24)
    for block in range(blocks):
        target, half = place(block)
        inner = total[span(block), :LANES] + gain * keys[span(block)].astype(jnp.float32)
        out_ref[target, half] = jnp.where(head, query[span(block)] * inner, inner).astype(jnp.bfloat16)


def activate_kernel(mixed_ref, query_ref, out_ref):
    groups, halves, channels, length = mixed_ref.shape
    rim = 6
    token = lax.broadcasted_iota(jnp.int32, (length, LANES), 0)
    for half in range(halves):
        inner = mixed_ref[:, half].reshape(groups * channels, length).astype(jnp.float32).T
        product = jnp.where(token < rim, inner, query_ref[half] * inner)
        out_ref[half * length : (half + 1) * length] = product.astype(jnp.bfloat16)


def project_kernel(index_ref, both_ref, own_weight_ref, other_weight_ref, out_ref):
    chips, _, width = out_ref.shape
    core = index_ref[1]
    lhs = jnp.concatenate([both_ref[core], both_ref[1 - core]], axis=1)
    for chip in range(chips):
        columns = pl.ds(pl.multiple_of((2 * chip + core) * width, width), width)
        weight = jnp.concatenate([own_weight_ref[:, columns], other_weight_ref[:, columns]], axis=0)
        out_ref[chip] = jnp.dot(lhs, weight, preferred_element_type=jnp.float32).astype(jnp.bfloat16)


def local(features, short_weight, long_filter, skip_gain, out_weight):
    pairs = lax.axis_size("ctx")
    chips = lax.axis_size("chip")
    length = features.shape[2]
    width = features.shape[4]
    channels = width // pairs
    order = [[(place + pairs // 2) % pairs for place in range(pairs)]]
    position = (lax.axis_index("ctx") + pairs // 2) % pairs
    index = jnp.stack([position, lax.axis_index("core")]).astype(jnp.int32)
    tiles = jnp.transpose(features, (0, 1, 3, 2, 4)).reshape(2, 3, length, width)
    taps = jnp.transpose(short_weight, (1, 0, 2))
    scalars = pl.BlockSpec(memory_space=pltpu.SMEM)
    vmem = pl.BlockSpec(memory_space=pltpu.VMEM)
    hbm = pl.BlockSpec(memory_space=pltpu.HBM)
    packed, weights, query = pl.pallas_call(
        pack_kernel,
        out_shape=(
            pltpu.VMEM((pairs, 5, channels, length), jnp.bfloat16),
            pltpu.VMEM((channels, LANES), jnp.float32),
            pltpu.VMEM((2, length, width), jnp.float32),
        ),
        in_specs=[scalars] + [hbm] * 4,
        out_specs=(vmem, vmem, vmem),
        scratch_shapes=[
            pltpu.VMEM((2, 3, length, width), jnp.bfloat16),
            pltpu.VMEM((2, length, width), jnp.bfloat16),
            pltpu.VMEM(taps.shape, jnp.bfloat16),
            pltpu.VMEM((1, width), jnp.float32),
            pltpu.VMEM((3, 8 + length, width), jnp.float32),
            pltpu.VMEM((LANES, LANES), jnp.float32),
            pltpu.VMEM((LANES, LANES), jnp.float32),
            pltpu.VMEM((LANES, LANES), jnp.float32),
            pltpu.SemaphoreType.DMA((5,)),
        ],
        compiler_params=pltpu.CompilerParams(vmem_limit_bytes=4 * MIB),
        cost_estimate=pl.CostEstimate(flops=1000000, bytes_accessed=600000, transcendentals=0),
        interpret=INTERPRET,
    )(
        index,
        in_hbm(tiles),
        in_hbm(long_filter.reshape(2, length, width)),
        in_hbm(taps),
        in_hbm(skip_gain.reshape(1, width)),
    )
    packed = lax.all_to_all(packed, "ctx", 0, 0, tiled=True, axis_index_groups=order)
    other_weight = lax.ppermute(out_weight, "core", [(0, 1), (1, 0)])
    forward, inverse = tables()
    rows = 2 * pairs * channels
    mixed = pl.pallas_call(
        mix_kernel,
        out_shape=pltpu.VMEM((pairs, 2, channels, length), jnp.bfloat16),
        in_specs=[vmem] * 2 + [hbm] * 2,
        out_specs=vmem,
        scratch_shapes=[
            pltpu.VMEM((rows, LANES), jnp.float32),
            pltpu.VMEM((rows, LANES), jnp.bfloat16),
            pltpu.VMEM((rows, LANES), jnp.bfloat16),
            pltpu.VMEM((rows, PERIOD), jnp.float32),
            pltpu.VMEM((rows, PERIOD), jnp.float32),
            pltpu.VMEM((3, rows, LANES), jnp.float32),
            pltpu.VMEM((rows, PERIOD), jnp.float32),
            pltpu.VMEM(forward.shape, jnp.bfloat16),
            pltpu.VMEM(inverse.shape, jnp.float32),
            pltpu.SemaphoreType.DMA((2,)),
        ],
        compiler_params=pltpu.CompilerParams(vmem_limit_bytes=6 * MIB),
        cost_estimate=pl.CostEstimate(flops=100000000, bytes_accessed=600000, transcendentals=0),
        interpret=INTERPRET,
    )(
        packed,
        weights,
        in_hbm(jnp.asarray(forward)),
        in_hbm(jnp.asarray(inverse)),
    )
    mixed = lax.all_to_all(mixed, "ctx", 0, 0, tiled=True, axis_index_groups=order)
    activated = pl.pallas_call(
        activate_kernel,
        out_shape=pltpu.VMEM((2 * length, width), jnp.bfloat16),
        in_specs=[vmem] * 2,
        out_specs=vmem,
        compiler_params=pltpu.CompilerParams(vmem_limit_bytes=4 * MIB),
        cost_estimate=pl.CostEstimate(flops=1000000, bytes_accessed=300000, transcendentals=0),
        interpret=INTERPRET,
    )(mixed, query)
    both = lax.all_gather(activated, "core", axis=0)
    partial = pl.pallas_call(
        project_kernel,
        out_shape=pltpu.VMEM((chips, 2 * length, width), jnp.bfloat16),
        in_specs=[scalars] + [vmem] * 3,
        out_specs=vmem,
        compiler_params=pltpu.CompilerParams(vmem_limit_bytes=8 * MIB),
        cost_estimate=pl.CostEstimate(flops=268435456, bytes_accessed=3300000, transcendentals=0),
        interpret=INTERPRET,
    )(index, both, out_weight, other_weight)
    shares = lax.all_to_all(partial, "chip", 0, 0, tiled=True)
    result = jnp.sum(shares.astype(jnp.float32), axis=0).astype(jnp.bfloat16)
    return result.reshape(2, 1, length, width)


def solution(mesh):
    pairs, parts = mesh.shape["ctx"], mesh.shape["ch"]
    split = Mesh(mesh.devices.reshape(pairs, parts // 2, 2), ("ctx", "chip", "core"))
    ch = ("chip", "core")
    in_specs = (
        P(None, "ctx", None, None, ch),
        P(None, None, ch),
        P(None, "ctx", None, ch),
        P(ch),
        P(ch, None),
    )
    return jax.shard_map(
        local, mesh=split, in_specs=in_specs, out_specs=P(None, "ctx", None, ch), check_vma=False
    )
```

```python
import math

import jax
import jax.numpy as jnp
import numpy as np
from jax import lax
from jax.experimental import pallas as pl
from jax.experimental.pallas import tpu as pltpu
from jax.sharding import Mesh, PartitionSpec as P

INTERPRET = False
MIB = 2**20
CTX_FIRST = 11
CHIP_FIRST = 14
LANES = 128
PERIOD = 2 * LANES


def in_hbm(value):
    return pltpu.with_memory_space_constraint(value, pltpu.HBM)


def tables():
    t = np.arange(LANES)[:, None]
    k = np.arange(LANES)[None, :]
    angle = 2.0 * math.pi * ((t * k) % PERIOD) / PERIOD
    sign = np.where(t % 2 == 0, 1.0, -1.0)
    cosine, sine = np.cos(angle), -np.sin(angle)
    forward = np.concatenate([cosine, np.where(k == 0, sign, sine)], axis=1)
    scale = np.where(k == 0, 1.0, 2.0) / PERIOD
    inverse = np.concatenate(
        [cosine * scale, np.where(k == 0, sign / PERIOD, sine * scale)], axis=1
    ).T
    high = forward.astype(jnp.bfloat16)
    low = (forward - high.astype(np.float64)).astype(jnp.bfloat16)
    return np.stack([high, low]), inverse.astype(np.float32)


def pack_kernel(
    index_ref, features_hbm, filter_hbm, taps_hbm, gain_hbm, out_ref, weights_ref, query_ref,
    features_ref, filter_ref, taps_ref, gain_ref, extended, edges, rows, turned, sems,
):
    groups = out_ref.shape[0]
    channels = LANES // groups
    streams = features_ref.shape[1]
    taps = taps_ref.shape[1]
    rim = taps - 1
    copies = [
        pltpu.make_async_copy(taps_hbm, taps_ref, sems.at[3]),
        pltpu.make_async_copy(features_hbm.at[0], features_ref.at[0], sems.at[0]),
        pltpu.make_async_copy(features_hbm.at[1], features_ref.at[1], sems.at[1]),
        pltpu.make_async_copy(filter_hbm, filter_ref, sems.at[2]),
        pltpu.make_async_copy(gain_hbm, gain_ref, sems.at[4]),
    ]
    for copy in copies:
        copy.start()

    def put(row, tile):
        out_ref[:, row] = tile.T.astype(jnp.bfloat16).reshape(groups, channels, LANES)

    extended[:, :8] = jnp.zeros((streams, 8, LANES), jnp.float32)
    edges[...] = jnp.zeros_like(edges)
    rows[...] = jnp.zeros_like(rows)
    copies[0].wait()
    for half in range(2):
        copies[1 + half].wait()
        featured = []
        for stream in range(streams):
            value = features_ref[half, stream].astype(jnp.float32)
            extended[stream, 8:] = value
            base = 2 * rim * (half * streams + stream)
            edges[base : base + rim] = extended[stream, 8 + LANES - rim : 8 + LANES]
            edges[base + rim : base + 2 * rim] = extended[stream, 8 : 8 + rim]
            summed = taps_ref[stream, 0:1].astype(jnp.float32) * value
            for i in range(1, taps):
                weight = taps_ref[stream, i : i + 1].astype(jnp.float32)
                summed = summed + weight * extended[stream, 8 - i : 8 - i + LANES]
            featured.append(summed)
        query_ref[half] = featured[0]
        put(half, featured[1] * featured[2])
    copies[3].wait()
    for half in range(2):
        put(2 + half, filter_ref[half].astype(jnp.float32))
    put(4, edges[...])
    copies[4].wait()
    for stream in range(streams):
        rows[stream * 8 : stream * 8 + taps] = taps_ref[stream].astype(jnp.float32)
    rows[streams * 8 : streams * 8 + 1] = gain_ref[...]
    turned[...] = rows[...].T
    first = pl.multiple_of(index_ref[0] * channels, channels)
    weights_ref[...] = turned[pl.ds(first, channels)]


def mix_kernel(
    packed_ref, weights_ref, forward_hbm, inverse_hbm, out_ref,
    query, keys, lags, key_spec, lag_spec, resp, total, forward_ref, inverse_ref, sems,
):
    forward_copy = pltpu.make_async_copy(forward_hbm, forward_ref, sems.at[0])
    inverse_copy = pltpu.make_async_copy(inverse_hbm, inverse_ref, sems.at[1])
    forward_copy.start()
    inverse_copy.start()
    pairs = packed_ref.shape[0]
    blocks = 2 * pairs
    channels = packed_ref.shape[2]
    streams, taps = 3, 7
    rim = taps - 1
    step = 2 * rim
    lane = lax.broadcasted_iota(jnp.int32, (channels, LANES), 1)

    def place(block):
        owner, half = (block, 0) if block < pairs else (blocks - 1 - block, 1)
        return (owner - CTX_FIRST) % pairs, half

    def span(block):
        return slice(block * channels, (block + 1) * channels)

    def column(index):
        return jnp.broadcast_to(weights_ref[:, index : index + 1], (channels, LANES))

    for block in range(blocks):
        source, half = place(block)
        lags[span(block)] = packed_ref[source, 2 + half]
    stream_of = lane // step % streams
    weight = [
        jnp.where(stream_of == 0, column(i), jnp.where(stream_of == 1, column(8 + i), column(16 + i)))
        for i in range(taps)
    ]
    tail = lane % step < rim
    lower = lane < streams * step
    edge = [packed_ref[place(owner)[0], 4].astype(jnp.float32) for owner in range(pairs)]
    head = lane < rim
    for owner in range(pairs):
        before = edge[owner - 1] if owner else jnp.zeros_like(edge[0])
        if owner + 1 < pairs:
            after = edge[owner + 1]
        else:
            after = pltpu.roll(edge[owner], streams * step, 1)
        value = jnp.where(tail, jnp.where(lower, before, after), edge[owner])
        summed = weight[0] * value
        for i in range(1, taps):
            summed = summed + weight[i] * pltpu.roll(value, i, 1)
        product = summed * pltpu.roll(summed, LANES - step, 1)
        for half, block in ((0, owner), (1, blocks - 1 - owner)):
            first = half * streams * step + rim
            gated = pltpu.roll(product, LANES - first - step, 1)
            whole = packed_ref[place(owner)[0], half].astype(jnp.float32)
            keys[span(block)] = jnp.where(head, gated, whole).astype(jnp.bfloat16)
            query[span(block)] = pltpu.roll(summed, LANES - first, 1)

    def transform(values):
        return jnp.dot(values, forward_ref[0], preferred_element_type=jnp.float32) + jnp.dot(
            values, forward_ref[1], preferred_element_type=jnp.float32
        )

    forward_copy.wait()
    key_spec[...] = transform(keys[...])
    lag_spec[...] = transform(lags[...])
    parity = jnp.where(lane % 2 == 0, 1.0, -1.0).astype(jnp.float32)
    for block in range(blocks):
        real = lag_spec[span(block), :LANES]
        imag = lag_spec[span(block), LANES:]
        if block:
            real = real + parity * lag_spec[span(block - 1), :LANES]
            imag = imag + parity * lag_spec[span(block - 1), LANES:]
        resp[0, span(block)] = real
        resp[1, span(block)] = jnp.where(lane == 0, 0.0, imag)
        resp[2, span(block)] = jnp.where(lane == 0, imag, real)
    group = 4
    for base in range(0, blocks, group):
        sums = [[None, None] for _ in range(group)]
        for block in range(base + group):
            real = key_spec[span(block), :LANES]
            imag = key_spec[span(block), LANES:]
            for j in range(group):
                gap = base + j - block
                if gap < 0:
                    continue
                first = resp[0, span(gap)]
                cross = resp[1, span(gap)]
                second = resp[2, span(gap)]
                out_real = real * first - imag * cross
                out_imag = real * cross + imag * second
                if sums[j][0] is None:
                    sums[j] = [out_real, out_imag]
                else:
                    sums[j] = [sums[j][0] + out_real, sums[j][1] + out_imag]
        for j in range(group):
            total[span(base + j), :LANES] = sums[j][0]
            total[span(base + j), LANES:] = sums[j][1]
    inverse_copy.wait()
    convolved = jnp.dot(
        total[...], inverse_ref[...], preferred_element_type=jnp.float32, precision=lax.Precision.HIGHEST
    )
    total[:, :LANES] = convolved
    gain = column(24)
    for block in range(blocks):
        target, half = place(block)
        inner = total[span(block), :LANES] + gain * keys[span(block)].astype(jnp.float32)
        out_ref[target, half] = jnp.where(head, query[span(block)] * inner, inner).astype(jnp.bfloat16)


def activate_kernel(mixed_ref, query_ref, out_ref):
    groups, halves, channels, length = mixed_ref.shape
    rim = 6
    token = lax.broadcasted_iota(jnp.int32, (length, LANES), 0)
    for half in range(halves):
        inner = mixed_ref[:, half].reshape(groups * channels, length).astype(jnp.float32).T
        product = jnp.where(token < rim, inner, query_ref[half] * inner)
        out_ref[half * length : (half + 1) * length] = product.astype(jnp.bfloat16)


def project_kernel(index_ref, both_ref, own_weight_ref, other_weight_ref, out_ref):
    chips, _, width = out_ref.shape
    core = index_ref[1]
    lhs = jnp.concatenate([both_ref[core], both_ref[1 - core]], axis=1)
    for chip in range(chips):
        block = 2 * ((chip + CHIP_FIRST) % chips) + core
        columns = pl.ds(pl.multiple_of(block * width, width), width)
        weight = jnp.concatenate([own_weight_ref[:, columns], other_weight_ref[:, columns]], axis=0)
        out_ref[chip] = jnp.dot(lhs, weight, preferred_element_type=jnp.float32).astype(jnp.bfloat16)


def local(features, short_weight, long_filter, skip_gain, out_weight):
    pairs = lax.axis_size("ctx")
    chips = lax.axis_size("chip")
    length = features.shape[2]
    width = features.shape[4]
    channels = width // pairs
    order = [[(place + CTX_FIRST) % pairs for place in range(pairs)]]
    chip_order = [[(place + CHIP_FIRST) % chips for place in range(chips)]]
    position = (lax.axis_index("ctx") + pairs - CTX_FIRST) % pairs
    index = jnp.stack([position, lax.axis_index("core")]).astype(jnp.int32)
    tiles = jnp.transpose(features, (0, 1, 3, 2, 4)).reshape(2, 3, length, width)
    taps = jnp.transpose(short_weight, (1, 0, 2))
    scalars = pl.BlockSpec(memory_space=pltpu.SMEM)
    vmem = pl.BlockSpec(memory_space=pltpu.VMEM)
    hbm = pl.BlockSpec(memory_space=pltpu.HBM)
    packed, weights, query = pl.pallas_call(
        pack_kernel,
        out_shape=(
            pltpu.VMEM((pairs, 5, channels, length), jnp.bfloat16),
            pltpu.VMEM((channels, LANES), jnp.float32),
            pltpu.VMEM((2, length, width), jnp.float32),
        ),
        in_specs=[scalars] + [hbm] * 4,
        out_specs=(vmem, vmem, vmem),
        scratch_shapes=[
            pltpu.VMEM((2, 3, length, width), jnp.bfloat16),
            pltpu.VMEM((2, length, width), jnp.bfloat16),
            pltpu.VMEM(taps.shape, jnp.bfloat16),
            pltpu.VMEM((1, width), jnp.float32),
            pltpu.VMEM((3, 8 + length, width), jnp.float32),
            pltpu.VMEM((LANES, LANES), jnp.float32),
            pltpu.VMEM((LANES, LANES), jnp.float32),
            pltpu.VMEM((LANES, LANES), jnp.float32),
            pltpu.SemaphoreType.DMA((5,)),
        ],
        compiler_params=pltpu.CompilerParams(vmem_limit_bytes=4 * MIB),
        cost_estimate=pl.CostEstimate(flops=1000000, bytes_accessed=600000, transcendentals=0),
        interpret=INTERPRET,
    )(
        index,
        in_hbm(tiles),
        in_hbm(long_filter.reshape(2, length, width)),
        in_hbm(taps),
        in_hbm(skip_gain.reshape(1, width)),
    )
    packed = lax.all_to_all(packed, "ctx", 0, 0, tiled=True, axis_index_groups=order)
    other_weight = lax.ppermute(out_weight, "core", [(0, 1), (1, 0)])
    forward, inverse = tables()
    rows = 2 * pairs * channels
    mixed = pl.pallas_call(
        mix_kernel,
        out_shape=pltpu.VMEM((pairs, 2, channels, length), jnp.bfloat16),
        in_specs=[vmem] * 2 + [hbm] * 2,
        out_specs=vmem,
        scratch_shapes=[
            pltpu.VMEM((rows, LANES), jnp.float32),
            pltpu.VMEM((rows, LANES), jnp.bfloat16),
            pltpu.VMEM((rows, LANES), jnp.bfloat16),
            pltpu.VMEM((rows, PERIOD), jnp.float32),
            pltpu.VMEM((rows, PERIOD), jnp.float32),
            pltpu.VMEM((3, rows, LANES), jnp.float32),
            pltpu.VMEM((rows, PERIOD), jnp.float32),
            pltpu.VMEM(forward.shape, jnp.bfloat16),
            pltpu.VMEM(inverse.shape, jnp.float32),
            pltpu.SemaphoreType.DMA((2,)),
        ],
        compiler_params=pltpu.CompilerParams(vmem_limit_bytes=6 * MIB),
        cost_estimate=pl.CostEstimate(flops=100000000, bytes_accessed=600000, transcendentals=0),
        interpret=INTERPRET,
    )(
        packed,
        weights,
        in_hbm(jnp.asarray(forward)),
        in_hbm(jnp.asarray(inverse)),
    )
    mixed = lax.all_to_all(mixed, "ctx", 0, 0, tiled=True, axis_index_groups=order)
    activated = pl.pallas_call(
        activate_kernel,
        out_shape=pltpu.VMEM((2 * length, width), jnp.bfloat16),
        in_specs=[vmem] * 2,
        out_specs=vmem,
        compiler_params=pltpu.CompilerParams(vmem_limit_bytes=4 * MIB),
        cost_estimate=pl.CostEstimate(flops=1000000, bytes_accessed=300000, transcendentals=0),
        interpret=INTERPRET,
    )(mixed, query)
    both = lax.all_gather(activated, "core", axis=0)
    partial = pl.pallas_call(
        project_kernel,
        out_shape=pltpu.VMEM((chips, 2 * length, width), jnp.bfloat16),
        in_specs=[scalars] + [vmem] * 3,
        out_specs=vmem,
        compiler_params=pltpu.CompilerParams(vmem_limit_bytes=8 * MIB),
        cost_estimate=pl.CostEstimate(flops=268435456, bytes_accessed=3300000, transcendentals=0),
        interpret=INTERPRET,
    )(index, both, out_weight, other_weight)
    shares = lax.all_to_all(partial, "chip", 0, 0, tiled=True, axis_index_groups=chip_order)
    result = jnp.sum(shares.astype(jnp.float32), axis=0).astype(jnp.bfloat16)
    return result.reshape(2, 1, length, width)


def solution(mesh):
    pairs, parts = mesh.shape["ctx"], mesh.shape["ch"]
    split = Mesh(mesh.devices.reshape(pairs, parts // 2, 2), ("ctx", "chip", "core"))
    ch = ("chip", "core")
    in_specs = (
        P(None, "ctx", None, None, ch),
        P(None, None, ch),
        P(None, "ctx", None, ch),
        P(ch),
        P(ch, None),
    )
    return jax.shard_map(
        local, mesh=split, in_specs=in_specs, out_specs=P(None, "ctx", None, ch), check_vma=False
    )
```

```python
import math

import jax
import jax.numpy as jnp
import numpy as np
from jax import lax
from jax.experimental import pallas as pl
from jax.experimental.pallas import tpu as pltpu
from jax.sharding import Mesh, PartitionSpec as P

INTERPRET = False
MIB = 2**20
CTX_FIRST = 11
CHIP_FIRST = 14
LANES = 128
PERIOD = 2 * LANES


def in_hbm(value):
    return pltpu.with_memory_space_constraint(value, pltpu.HBM)


def tables():
    t = np.arange(LANES)[:, None]
    k = np.arange(LANES)[None, :]
    angle = 2.0 * math.pi * ((t * k) % PERIOD) / PERIOD
    sign = np.where(t % 2 == 0, 1.0, -1.0)
    cosine, sine = np.cos(angle), -np.sin(angle)
    forward = np.concatenate([cosine, np.where(k == 0, sign, sine)], axis=1)
    scale = np.where(k == 0, 1.0, 2.0) / PERIOD
    inverse = np.concatenate(
        [cosine * scale, np.where(k == 0, sign / PERIOD, sine * scale)], axis=1
    ).T

    def split(table, axis):
        high = table.astype(jnp.bfloat16)
        low = (table - high.astype(np.float64)).astype(jnp.bfloat16)
        return np.concatenate([high, low], axis=axis)

    return split(forward, 0), split(inverse, 1)


def pack_kernel(
    index_ref, features_hbm, filter_hbm, taps_hbm, gain_hbm, out_ref, weights_ref, query_ref,
    features_ref, filter_ref, taps_ref, gain_ref, extended, edges, rows, turned, sems,
):
    groups = out_ref.shape[0]
    channels = LANES // groups
    streams = features_ref.shape[1]
    taps = taps_ref.shape[1]
    rim = taps - 1
    copies = [
        pltpu.make_async_copy(taps_hbm, taps_ref, sems.at[3]),
        pltpu.make_async_copy(features_hbm.at[0], features_ref.at[0], sems.at[0]),
        pltpu.make_async_copy(features_hbm.at[1], features_ref.at[1], sems.at[1]),
        pltpu.make_async_copy(filter_hbm, filter_ref, sems.at[2]),
        pltpu.make_async_copy(gain_hbm, gain_ref, sems.at[4]),
    ]
    for copy in copies:
        copy.start()

    def put(row, tile):
        out_ref[:, row] = tile.T.astype(jnp.bfloat16).reshape(groups, channels, LANES)

    extended[:, :8] = jnp.zeros((streams, 8, LANES), jnp.float32)
    edges[...] = jnp.zeros_like(edges)
    rows[...] = jnp.zeros_like(rows)
    copies[0].wait()
    for half in range(2):
        copies[1 + half].wait()
        featured = []
        for stream in range(streams):
            value = features_ref[half, stream].astype(jnp.float32)
            extended[stream, 8:] = value
            base = 2 * rim * (half * streams + stream)
            edges[base : base + rim] = extended[stream, 8 + LANES - rim : 8 + LANES]
            edges[base + rim : base + 2 * rim] = extended[stream, 8 : 8 + rim]
            summed = taps_ref[stream, 0:1].astype(jnp.float32) * value
            for i in range(1, taps):
                weight = taps_ref[stream, i : i + 1].astype(jnp.float32)
                summed = summed + weight * extended[stream, 8 - i : 8 - i + LANES]
            featured.append(summed)
        query_ref[half] = featured[0]
        put(half, featured[1] * featured[2])
    copies[3].wait()
    for half in range(2):
        put(2 + half, filter_ref[half].astype(jnp.float32))
    put(4, edges[...])
    copies[4].wait()
    for stream in range(streams):
        rows[stream * 8 : stream * 8 + taps] = taps_ref[stream].astype(jnp.float32)
    rows[streams * 8 : streams * 8 + 1] = gain_ref[...]
    turned[...] = rows[...].T
    first = pl.multiple_of(index_ref[0] * channels, channels)
    weights_ref[...] = turned[pl.ds(first, channels)]


def mix_kernel(
    index_ref, packed_ref, weights_ref, forward_hbm, inverse_hbm, matrix_hbm, out_ref, matrix_ref,
    query, keys, lags, key_spec, lag_spec, resp, total, forward_ref, inverse_ref, sems,
):
    forward_copy = pltpu.make_async_copy(forward_hbm, forward_ref, sems.at[0])
    inverse_copy = pltpu.make_async_copy(inverse_hbm, inverse_ref, sems.at[1])
    forward_copy.start()
    inverse_copy.start()
    chips = matrix_ref.shape[0]
    matrix_copies = []
    for chip in range(chips):
        block = 2 * ((chip + CHIP_FIRST) % chips) + index_ref[1]
        columns = pl.ds(pl.multiple_of(block * LANES, LANES), LANES)
        copy = pltpu.make_async_copy(matrix_hbm.at[:, columns], matrix_ref.at[chip], sems.at[2 + chip])
        copy.start()
        matrix_copies.append(copy)
    pairs = packed_ref.shape[0]
    blocks = 2 * pairs
    channels = packed_ref.shape[2]
    streams, taps = 3, 7
    rim = taps - 1
    step = 2 * rim
    lane = lax.broadcasted_iota(jnp.int32, (channels, LANES), 1)

    def place(block):
        owner, half = (block, 0) if block < pairs else (blocks - 1 - block, 1)
        return (owner - CTX_FIRST) % pairs, half

    def span(block):
        return slice(block * channels, (block + 1) * channels)

    def column(index):
        return jnp.broadcast_to(weights_ref[:, index : index + 1], (channels, LANES))

    for block in range(blocks):
        source, half = place(block)
        lags[span(block)] = packed_ref[source, 2 + half]
    stream_of = lane // step % streams
    weight = [
        jnp.where(stream_of == 0, column(i), jnp.where(stream_of == 1, column(8 + i), column(16 + i)))
        for i in range(taps)
    ]
    tail = lane % step < rim
    lower = lane < streams * step
    edge = [packed_ref[place(owner)[0], 4].astype(jnp.float32) for owner in range(pairs)]
    head = lane < rim
    for owner in range(pairs):
        before = edge[owner - 1] if owner else jnp.zeros_like(edge[0])
        if owner + 1 < pairs:
            after = edge[owner + 1]
        else:
            after = pltpu.roll(edge[owner], streams * step, 1)
        value = jnp.where(tail, jnp.where(lower, before, after), edge[owner])
        summed = weight[0] * value
        for i in range(1, taps):
            summed = summed + weight[i] * pltpu.roll(value, i, 1)
        product = summed * pltpu.roll(summed, LANES - step, 1)
        for half, block in ((0, owner), (1, blocks - 1 - owner)):
            first = half * streams * step + rim
            gated = pltpu.roll(product, LANES - first - step, 1)
            whole = packed_ref[place(owner)[0], half].astype(jnp.float32)
            keys[span(block)] = jnp.where(head, gated, whole).astype(jnp.bfloat16)
            query[span(block)] = pltpu.roll(summed, LANES - first, 1)

    def transform(values):
        return jnp.dot(
            jnp.concatenate([values, values], axis=1), forward_ref[...], preferred_element_type=jnp.float32
        )

    forward_copy.wait()
    key_spec[...] = transform(keys[...])
    lag_spec[...] = transform(lags[...])
    parity = jnp.where(lane % 2 == 0, 1.0, -1.0).astype(jnp.float32)
    for block in range(blocks):
        real = lag_spec[span(block), :LANES]
        imag = lag_spec[span(block), LANES:]
        if block:
            real = real + parity * lag_spec[span(block - 1), :LANES]
            imag = imag + parity * lag_spec[span(block - 1), LANES:]
        cross = jnp.where(lane == 0, 0.0, imag)
        resp[0, span(block)] = real + cross
        resp[1, span(block)] = cross
        resp[2, span(block)] = jnp.where(lane == 0, imag, real) - cross
    group = 4
    for base in range(0, blocks, group):
        sums = [None] * group
        for block in range(base + group):
            real = key_spec[span(block), :LANES]
            imag = key_spec[span(block), LANES:]
            both = real + imag
            for j in range(group):
                gap = base + j - block
                if gap < 0:
                    continue
                terms = [
                    real * resp[0, span(gap)],
                    both * resp[1, span(gap)],
                    imag * resp[2, span(gap)],
                ]
                if sums[j] is not None:
                    terms = [one + other for one, other in zip(sums[j], terms)]
                sums[j] = terms
        for j in range(group):
            total[span(base + j), :LANES] = sums[j][0] - sums[j][1]
            total[span(base + j), LANES:] = sums[j][1] + sums[j][2]
    inverse_copy.wait()
    high = total[...].astype(jnp.bfloat16)
    low = (total[...] - high.astype(jnp.float32)).astype(jnp.bfloat16)
    wide = jnp.dot(high, inverse_ref[...], preferred_element_type=jnp.float32)
    narrow = jnp.dot(low, inverse_ref[:, :LANES], preferred_element_type=jnp.float32)
    total[:, :LANES] = wide[:, :LANES] + (wide[:, LANES:] + narrow)
    gain = column(24)
    for block in range(blocks):
        target, half = place(block)
        inner = total[span(block), :LANES] + gain * keys[span(block)].astype(jnp.float32)
        out_ref[target, half] = jnp.where(head, query[span(block)] * inner, inner).astype(jnp.bfloat16)
    for copy in matrix_copies:
        copy.wait()


def activate_kernel(mixed_ref, query_ref, out_ref):
    groups, halves, channels, length = mixed_ref.shape
    rim = 6
    token = lax.broadcasted_iota(jnp.int32, (length, LANES), 0)
    for half in range(halves):
        inner = mixed_ref[:, half].reshape(groups * channels, length).astype(jnp.float32).T
        product = jnp.where(token < rim, inner, query_ref[half] * inner)
        out_ref[half * length : (half + 1) * length] = product.astype(jnp.bfloat16)


def project_kernel(index_ref, both_ref, own_weight_ref, other_weight_ref, out_ref):
    chips, _, width = out_ref.shape
    core = index_ref[1]
    lhs = jnp.concatenate([both_ref[core], both_ref[1 - core]], axis=1)

    def columns(chip):
        block = 2 * ((chip + CHIP_FIRST) % chips) + core
        other = other_weight_ref[:, pl.ds(pl.multiple_of(block * width, width), width)]
        return jnp.concatenate([own_weight_ref[chip], other], axis=0)

    step = math.gcd(chips, 2)
    for first in range(0, chips, step):
        weight = jnp.concatenate([columns(first + i) for i in range(step)], axis=1)
        product = jnp.dot(lhs, weight, preferred_element_type=jnp.float32).astype(jnp.bfloat16)
        for i in range(step):
            out_ref[first + i] = product[:, i * width : (i + 1) * width]


def local(features, short_weight, long_filter, skip_gain, out_weight):
    pairs = lax.axis_size("ctx")
    chips = lax.axis_size("chip")
    length = features.shape[2]
    width = features.shape[4]
    channels = width // pairs
    order = [[(place + CTX_FIRST) % pairs for place in range(pairs)]]
    chip_order = [[(place + CHIP_FIRST) % chips for place in range(chips)]]
    position = (lax.axis_index("ctx") + pairs - CTX_FIRST) % pairs
    index = jnp.stack([position, lax.axis_index("core")]).astype(jnp.int32)
    tiles = jnp.transpose(features, (0, 1, 3, 2, 4)).reshape(2, 3, length, width)
    taps = jnp.transpose(short_weight, (1, 0, 2))
    scalars = pl.BlockSpec(memory_space=pltpu.SMEM)
    vmem = pl.BlockSpec(memory_space=pltpu.VMEM)
    hbm = pl.BlockSpec(memory_space=pltpu.HBM)
    packed, weights, query = pl.pallas_call(
        pack_kernel,
        out_shape=(
            pltpu.VMEM((pairs, 5, channels, length), jnp.bfloat16),
            pltpu.VMEM((channels, LANES), jnp.float32),
            pltpu.VMEM((2, length, width), jnp.float32),
        ),
        in_specs=[scalars] + [hbm] * 4,
        out_specs=(vmem, vmem, vmem),
        scratch_shapes=[
            pltpu.VMEM((2, 3, length, width), jnp.bfloat16),
            pltpu.VMEM((2, length, width), jnp.bfloat16),
            pltpu.VMEM(taps.shape, jnp.bfloat16),
            pltpu.VMEM((1, width), jnp.float32),
            pltpu.VMEM((3, 8 + length, width), jnp.float32),
            pltpu.VMEM((LANES, LANES), jnp.float32),
            pltpu.VMEM((LANES, LANES), jnp.float32),
            pltpu.VMEM((LANES, LANES), jnp.float32),
            pltpu.SemaphoreType.DMA((5,)),
        ],
        compiler_params=pltpu.CompilerParams(vmem_limit_bytes=4 * MIB),
        cost_estimate=pl.CostEstimate(flops=1000000, bytes_accessed=600000, transcendentals=0),
        interpret=INTERPRET,
    )(
        index,
        in_hbm(tiles),
        in_hbm(long_filter.reshape(2, length, width)),
        in_hbm(taps),
        in_hbm(skip_gain.reshape(1, width)),
    )
    packed = lax.all_to_all(packed, "ctx", 0, 0, tiled=True, axis_index_groups=order)
    other_weight = lax.ppermute(out_weight, "core", [(0, 1), (1, 0)])
    forward, inverse = tables()
    rows = 2 * pairs * channels
    mixed, own_weight = pl.pallas_call(
        mix_kernel,
        out_shape=(
            pltpu.VMEM((pairs, 2, channels, length), jnp.bfloat16),
            pltpu.VMEM((chips, width, width), jnp.bfloat16),
        ),
        in_specs=[scalars] + [vmem] * 2 + [hbm] * 3,
        out_specs=(vmem, vmem),
        scratch_shapes=[
            pltpu.VMEM((rows, LANES), jnp.float32),
            pltpu.VMEM((rows, LANES), jnp.bfloat16),
            pltpu.VMEM((rows, LANES), jnp.bfloat16),
            pltpu.VMEM((rows, PERIOD), jnp.float32),
            pltpu.VMEM((rows, PERIOD), jnp.float32),
            pltpu.VMEM((3, rows, LANES), jnp.float32),
            pltpu.VMEM((rows, PERIOD), jnp.float32),
            pltpu.VMEM(forward.shape, jnp.bfloat16),
            pltpu.VMEM(inverse.shape, jnp.bfloat16),
            pltpu.SemaphoreType.DMA((2 + chips,)),
        ],
        compiler_params=pltpu.CompilerParams(vmem_limit_bytes=6 * MIB),
        cost_estimate=pl.CostEstimate(flops=100000000, bytes_accessed=600000, transcendentals=0),
        interpret=INTERPRET,
    )(
        index,
        packed,
        weights,
        in_hbm(jnp.asarray(forward)),
        in_hbm(jnp.asarray(inverse)),
        in_hbm(out_weight),
    )
    mixed = lax.all_to_all(mixed, "ctx", 0, 0, tiled=True, axis_index_groups=order)
    activated = pl.pallas_call(
        activate_kernel,
        out_shape=pltpu.VMEM((2 * length, width), jnp.bfloat16),
        in_specs=[vmem] * 2,
        out_specs=vmem,
        compiler_params=pltpu.CompilerParams(vmem_limit_bytes=4 * MIB),
        cost_estimate=pl.CostEstimate(flops=1000000, bytes_accessed=300000, transcendentals=0),
        interpret=INTERPRET,
    )(mixed, query)
    both = lax.all_gather(activated, "core", axis=0)
    partial = pl.pallas_call(
        project_kernel,
        out_shape=pltpu.VMEM((chips, 2 * length, width), jnp.bfloat16),
        in_specs=[scalars] + [vmem] * 3,
        out_specs=vmem,
        compiler_params=pltpu.CompilerParams(vmem_limit_bytes=8 * MIB),
        cost_estimate=pl.CostEstimate(flops=268435456, bytes_accessed=3300000, transcendentals=0),
        interpret=INTERPRET,
    )(index, both, own_weight, other_weight)
    shares = lax.all_to_all(partial, "chip", 0, 0, tiled=True, axis_index_groups=chip_order)
    result = jnp.sum(shares.astype(jnp.float32), axis=0).astype(jnp.bfloat16)
    return result.reshape(2, 1, length, width)


def solution(mesh):
    pairs, parts = mesh.shape["ctx"], mesh.shape["ch"]
    split = Mesh(mesh.devices.reshape(pairs, parts // 2, 2), ("ctx", "chip", "core"))
    ch = ("chip", "core")
    in_specs = (
        P(None, "ctx", None, None, ch),
        P(None, None, ch),
        P(None, "ctx", None, ch),
        P(ch),
        P(ch, None),
    )
    return jax.shard_map(
        local, mesh=split, in_specs=in_specs, out_specs=P(None, "ctx", None, ch), check_vma=False
    )
```

```python
import math

import jax
import jax.numpy as jnp
import numpy as np
from jax import lax
from jax.experimental import pallas as pl
from jax.experimental.pallas import tpu as pltpu
from jax.sharding import Mesh, PartitionSpec as P

INTERPRET = False
MIB = 2**20
CTX_FIRST = 11
LANES = 128
PERIOD = 2 * LANES


def row_first(side):
    return side - 1


def part_first(parts):
    return parts - 2


def rotated(first, count):
    return [[(place + first) % count for place in range(count)]]


def in_hbm(value):
    return pltpu.with_memory_space_constraint(value, pltpu.HBM)


def tables():
    t = np.arange(LANES)[:, None]
    k = np.arange(LANES)[None, :]
    angle = 2.0 * math.pi * ((t * k) % PERIOD) / PERIOD
    sign = np.where(t % 2 == 0, 1.0, -1.0)
    cosine, sine = np.cos(angle), -np.sin(angle)
    forward = np.concatenate([cosine, np.where(k == 0, sign, sine)], axis=1)
    scale = np.where(k == 0, 1.0, 2.0) / PERIOD
    inverse = np.concatenate(
        [cosine * scale, np.where(k == 0, sign / PERIOD, sine * scale)], axis=1
    ).T

    def split(table, axis):
        high = table.astype(jnp.bfloat16)
        low = (table - high.astype(np.float64)).astype(jnp.bfloat16)
        return np.concatenate([high, low], axis=axis)

    return split(forward, 0), split(inverse, 1)


def pack_kernel(
    index_ref, features_hbm, filter_hbm, taps_hbm, gain_hbm, out_ref, weights_ref, query_ref,
    features_ref, filter_ref, taps_ref, gain_ref, extended, edges, rows, turned, sems,
):
    groups = out_ref.shape[0]
    channels = LANES // groups
    streams = features_ref.shape[1]
    taps = taps_ref.shape[1]
    rim = taps - 1
    copies = [
        pltpu.make_async_copy(taps_hbm, taps_ref, sems.at[3]),
        pltpu.make_async_copy(features_hbm.at[0], features_ref.at[0], sems.at[0]),
        pltpu.make_async_copy(features_hbm.at[1], features_ref.at[1], sems.at[1]),
        pltpu.make_async_copy(filter_hbm, filter_ref, sems.at[2]),
        pltpu.make_async_copy(gain_hbm, gain_ref, sems.at[4]),
    ]
    for copy in copies:
        copy.start()

    def put(row, tile):
        out_ref[:, row] = tile.T.astype(jnp.bfloat16).reshape(groups, channels, LANES)

    extended[:, :8] = jnp.zeros((streams, 8, LANES), jnp.float32)
    edges[...] = jnp.zeros_like(edges)
    rows[...] = jnp.zeros_like(rows)
    copies[0].wait()
    for half in range(2):
        copies[1 + half].wait()
        featured = []
        for stream in range(streams):
            value = features_ref[half, stream].astype(jnp.float32)
            extended[stream, 8:] = value
            base = 2 * rim * (half * streams + stream)
            edges[base : base + rim] = extended[stream, 8 + LANES - rim : 8 + LANES]
            edges[base + rim : base + 2 * rim] = extended[stream, 8 : 8 + rim]
            summed = taps_ref[stream, 0:1].astype(jnp.float32) * value
            for i in range(1, taps):
                weight = taps_ref[stream, i : i + 1].astype(jnp.float32)
                summed = summed + weight * extended[stream, 8 - i : 8 - i + LANES]
            featured.append(summed)
        query_ref[half] = featured[0]
        put(half, featured[1] * featured[2])
    copies[3].wait()
    for half in range(2):
        put(2 + half, filter_ref[half].astype(jnp.float32))
    put(4, edges[...])
    copies[4].wait()
    for stream in range(streams):
        rows[stream * 8 : stream * 8 + taps] = taps_ref[stream].astype(jnp.float32)
    rows[streams * 8 : streams * 8 + 1] = gain_ref[...]
    turned[...] = rows[...].T
    first = pl.multiple_of(index_ref[0] * channels, channels)
    weights_ref[...] = turned[pl.ds(first, channels)]


def mix_kernel(
    packed_ref, weights_ref, forward_hbm, inverse_hbm, out_ref,
    query, keys, lags, key_spec, lag_spec, resp, total, forward_ref, inverse_ref, sems,
):
    forward_copy = pltpu.make_async_copy(forward_hbm, forward_ref, sems.at[0])
    inverse_copy = pltpu.make_async_copy(inverse_hbm, inverse_ref, sems.at[1])
    forward_copy.start()
    inverse_copy.start()
    pairs = packed_ref.shape[0]
    blocks = 2 * pairs
    channels = packed_ref.shape[2]
    streams, taps = 3, 7
    rim = taps - 1
    step = 2 * rim
    lane = lax.broadcasted_iota(jnp.int32, (channels, LANES), 1)

    def place(block):
        owner, half = (block, 0) if block < pairs else (blocks - 1 - block, 1)
        return (owner - CTX_FIRST) % pairs, half

    def span(block):
        return slice(block * channels, (block + 1) * channels)

    def column(index):
        return jnp.broadcast_to(weights_ref[:, index : index + 1], (channels, LANES))

    for block in range(blocks):
        source, half = place(block)
        lags[span(block)] = packed_ref[source, 2 + half]
    stream_of = lane // step % streams
    weight = [
        jnp.where(stream_of == 0, column(i), jnp.where(stream_of == 1, column(8 + i), column(16 + i)))
        for i in range(taps)
    ]
    tail = lane % step < rim
    lower = lane < streams * step
    edge = [packed_ref[place(owner)[0], 4].astype(jnp.float32) for owner in range(pairs)]
    head = lane < rim
    for owner in range(pairs):
        before = edge[owner - 1] if owner else jnp.zeros_like(edge[0])
        if owner + 1 < pairs:
            after = edge[owner + 1]
        else:
            after = pltpu.roll(edge[owner], streams * step, 1)
        value = jnp.where(tail, jnp.where(lower, before, after), edge[owner])
        summed = weight[0] * value
        for i in range(1, taps):
            summed = summed + weight[i] * pltpu.roll(value, i, 1)
        product = summed * pltpu.roll(summed, LANES - step, 1)
        for half, block in ((0, owner), (1, blocks - 1 - owner)):
            first = half * streams * step + rim
            gated = pltpu.roll(product, LANES - first - step, 1)
            whole = packed_ref[place(owner)[0], half].astype(jnp.float32)
            keys[span(block)] = jnp.where(head, gated, whole).astype(jnp.bfloat16)
            query[span(block)] = pltpu.roll(summed, LANES - first, 1)

    def transform(values):
        return jnp.dot(
            jnp.concatenate([values, values], axis=1), forward_ref[...], preferred_element_type=jnp.float32
        )

    forward_copy.wait()
    key_spec[...] = transform(keys[...])
    lag_spec[...] = transform(lags[...])
    parity = jnp.where(lane % 2 == 0, 1.0, -1.0).astype(jnp.float32)
    for block in range(blocks):
        real = lag_spec[span(block), :LANES]
        imag = lag_spec[span(block), LANES:]
        if block:
            real = real + parity * lag_spec[span(block - 1), :LANES]
            imag = imag + parity * lag_spec[span(block - 1), LANES:]
        cross = jnp.where(lane == 0, 0.0, imag)
        resp[0, span(block)] = real + cross
        resp[1, span(block)] = cross
        resp[2, span(block)] = jnp.where(lane == 0, imag, real) - cross
    group = 4
    for base in range(0, blocks, group):
        sums = [None] * group
        for block in range(base + group):
            real = key_spec[span(block), :LANES]
            imag = key_spec[span(block), LANES:]
            both = real + imag
            for j in range(group):
                gap = base + j - block
                if gap < 0:
                    continue
                terms = [
                    real * resp[0, span(gap)],
                    both * resp[1, span(gap)],
                    imag * resp[2, span(gap)],
                ]
                if sums[j] is not None:
                    terms = [one + other for one, other in zip(sums[j], terms)]
                sums[j] = terms
        for j in range(group):
            total[span(base + j), :LANES] = sums[j][0] - sums[j][1]
            total[span(base + j), LANES:] = sums[j][1] + sums[j][2]
    inverse_copy.wait()
    high = total[...].astype(jnp.bfloat16)
    low = (total[...] - high.astype(jnp.float32)).astype(jnp.bfloat16)
    wide = jnp.dot(high, inverse_ref[...], preferred_element_type=jnp.float32)
    narrow = jnp.dot(low, inverse_ref[:, :LANES], preferred_element_type=jnp.float32)
    total[:, :LANES] = wide[:, :LANES] + (wide[:, LANES:] + narrow)
    gain = column(24)
    for block in range(blocks):
        target, half = place(block)
        inner = total[span(block), :LANES] + gain * keys[span(block)].astype(jnp.float32)
        out_ref[target, half] = jnp.where(head, query[span(block)] * inner, inner).astype(jnp.bfloat16)


def activate_kernel(mixed_ref, query_ref, out_ref):
    groups, halves, channels, length = mixed_ref.shape
    rim = 6
    token = lax.broadcasted_iota(jnp.int32, (length, LANES), 0)
    for half in range(halves):
        inner = mixed_ref[:, half].reshape(groups * channels, length).astype(jnp.float32).T
        product = jnp.where(token < rim, inner, query_ref[half] * inner)
        for copy in range(out_ref.shape[0]):
            out_ref[copy, half * length : (half + 1) * length] = product.astype(jnp.bfloat16)


def divide_kernel(index_ref, weight_hbm, *refs):
    pieces, sems = refs[:-1], refs[-1]
    side = len(pieces)
    share = pieces[0].shape[1]
    copies = []
    for step, piece in enumerate(pieces):
        columns = pl.ds(pl.multiple_of((index_ref[1] + step) % side * share, share), share)
        copies.append(pltpu.make_async_copy(weight_hbm.at[:, columns], piece, sems.at[step]))
    for copy in copies:
        copy.start()
    for copy in copies:
        copy.wait()


def arrange_kernel(index_ref, row_ref, out_ref):
    side, _, width = row_ref.shape
    shift = row_first(side)
    for step in range(side):
        source = (index_ref[1] + (2 * side - step - shift)) % side
        out_ref[:, step * width : (step + 1) * width] = row_ref[source]


def project_kernel(lhs_ref, *refs):
    weights, out_ref = refs[:-1], refs[-1]
    parts, _, width = out_ref.shape
    lhs = lhs_ref[...]
    for part in range(0, parts, 2):
        columns = slice(part * width, (part + 2) * width)
        weight = jnp.concatenate([piece[:, columns] for piece in weights], axis=0)
        product = jnp.dot(lhs, weight, preferred_element_type=jnp.float32).astype(jnp.bfloat16)
        for i in range(2):
            place = (part + i - part_first(parts)) % parts
            out_ref[place] = product[:, i * width : (i + 1) * width]


def local(features, short_weight, long_filter, skip_gain, out_weight):
    pairs = lax.axis_size("ctx")
    side = lax.axis_size("x")
    parts = 2 * lax.axis_size("y")
    length = features.shape[2]
    width = features.shape[4]
    channels = width // pairs
    order = rotated(CTX_FIRST, pairs)
    position = (lax.axis_index("ctx") + pairs - CTX_FIRST) % pairs
    index = jnp.stack([position, lax.axis_index("x")]).astype(jnp.int32)
    tiles = jnp.transpose(features, (0, 1, 3, 2, 4)).reshape(2, 3, length, width)
    taps = jnp.transpose(short_weight, (1, 0, 2))
    scalars = pl.BlockSpec(memory_space=pltpu.SMEM)
    vmem = pl.BlockSpec(memory_space=pltpu.VMEM)
    hbm = pl.BlockSpec(memory_space=pltpu.HBM)
    packed, weights, query = pl.pallas_call(
        pack_kernel,
        out_shape=(
            pltpu.VMEM((pairs, 5, channels, length), jnp.bfloat16),
            pltpu.VMEM((channels, LANES), jnp.float32),
            pltpu.VMEM((2, length, width), jnp.float32),
        ),
        in_specs=[scalars] + [hbm] * 4,
        out_specs=(vmem, vmem, vmem),
        scratch_shapes=[
            pltpu.VMEM((2, 3, length, width), jnp.bfloat16),
            pltpu.VMEM((2, length, width), jnp.bfloat16),
            pltpu.VMEM(taps.shape, jnp.bfloat16),
            pltpu.VMEM((1, width), jnp.float32),
            pltpu.VMEM((3, 8 + length, width), jnp.float32),
            pltpu.VMEM((LANES, LANES), jnp.float32),
            pltpu.VMEM((LANES, LANES), jnp.float32),
            pltpu.VMEM((LANES, LANES), jnp.float32),
            pltpu.SemaphoreType.DMA((5,)),
        ],
        compiler_params=pltpu.CompilerParams(vmem_limit_bytes=4 * MIB),
        cost_estimate=pl.CostEstimate(flops=1000000, bytes_accessed=600000, transcendentals=0),
        interpret=INTERPRET,
    )(
        index,
        in_hbm(tiles),
        in_hbm(long_filter.reshape(2, length, width)),
        in_hbm(taps),
        in_hbm(skip_gain.reshape(1, width)),
    )
    packed = lax.all_to_all(packed, "ctx", 0, 0, tiled=True, axis_index_groups=order)
    pieces = pl.pallas_call(
        divide_kernel,
        out_shape=(jax.ShapeDtypeStruct((width, parts * width), jnp.bfloat16),) * side,
        in_specs=[scalars, hbm],
        out_specs=(vmem,) * side,
        scratch_shapes=[pltpu.SemaphoreType.DMA((side,))],
        compiler_params=pltpu.CompilerParams(vmem_limit_bytes=4 * MIB),
        cost_estimate=pl.CostEstimate(flops=0, bytes_accessed=2 * MIB, transcendentals=0),
        interpret=INTERPRET,
    )(index, in_hbm(out_weight))
    pieces = [pieces[0]] + [
        lax.ppermute(pieces[step], "x", [(source, (source + step) % side) for source in range(side)])
        for step in range(1, side)
    ]
    forward, inverse = tables()
    rows = 2 * pairs * channels
    mixed = pl.pallas_call(
        mix_kernel,
        out_shape=pltpu.VMEM((pairs, 2, channels, length), jnp.bfloat16),
        in_specs=[vmem] * 2 + [hbm] * 2,
        out_specs=vmem,
        scratch_shapes=[
            pltpu.VMEM((rows, LANES), jnp.float32),
            pltpu.VMEM((rows, LANES), jnp.bfloat16),
            pltpu.VMEM((rows, LANES), jnp.bfloat16),
            pltpu.VMEM((rows, PERIOD), jnp.float32),
            pltpu.VMEM((rows, PERIOD), jnp.float32),
            pltpu.VMEM((3, rows, LANES), jnp.float32),
            pltpu.VMEM((rows, PERIOD), jnp.float32),
            pltpu.VMEM(forward.shape, jnp.bfloat16),
            pltpu.VMEM(inverse.shape, jnp.bfloat16),
            pltpu.SemaphoreType.DMA((2,)),
        ],
        compiler_params=pltpu.CompilerParams(vmem_limit_bytes=6 * MIB),
        cost_estimate=pl.CostEstimate(flops=100000000, bytes_accessed=600000, transcendentals=0),
        interpret=INTERPRET,
    )(
        packed,
        weights,
        in_hbm(jnp.asarray(forward)),
        in_hbm(jnp.asarray(inverse)),
    )
    mixed = lax.all_to_all(mixed, "ctx", 0, 0, tiled=True, axis_index_groups=order)
    activated = pl.pallas_call(
        activate_kernel,
        out_shape=pltpu.VMEM((side, 2 * length, width), jnp.bfloat16),
        in_specs=[vmem] * 2,
        out_specs=vmem,
        compiler_params=pltpu.CompilerParams(vmem_limit_bytes=4 * MIB),
        cost_estimate=pl.CostEstimate(flops=1000000, bytes_accessed=300000, transcendentals=0),
        interpret=INTERPRET,
    )(mixed, query)
    row = lax.all_to_all(
        activated, "x", 0, 0, tiled=True, axis_index_groups=rotated(row_first(side), side)
    )
    lhs = pl.pallas_call(
        arrange_kernel,
        out_shape=pltpu.VMEM((2 * length, side * width), jnp.bfloat16),
        in_specs=[scalars, vmem],
        out_specs=vmem,
        compiler_params=pltpu.CompilerParams(vmem_limit_bytes=4 * MIB),
        cost_estimate=pl.CostEstimate(flops=0, bytes_accessed=500000, transcendentals=0),
        interpret=INTERPRET,
    )(index, row)
    partial = pl.pallas_call(
        project_kernel,
        out_shape=pltpu.VMEM((parts, 2 * length, width), jnp.bfloat16),
        in_specs=[vmem] * (1 + side),
        out_specs=vmem,
        compiler_params=pltpu.CompilerParams(vmem_limit_bytes=8 * MIB),
        cost_estimate=pl.CostEstimate(flops=268435456, bytes_accessed=3300000, transcendentals=0),
        interpret=INTERPRET,
    )(lhs, *pieces)
    shares = lax.all_to_all(
        partial, ("y", "core"), 0, 0, tiled=True, axis_index_groups=rotated(part_first(parts), parts)
    )
    result = jnp.sum(shares.astype(jnp.float32), axis=0).astype(jnp.bfloat16)
    return result.reshape(2, 1, length, width)


def solution(mesh):
    pairs, parts = mesh.shape["ctx"], mesh.shape["ch"]
    side = math.isqrt(parts // 2)
    split = Mesh(mesh.devices.reshape(pairs, side, side, 2), ("ctx", "x", "y", "core"))
    ch = ("x", "y", "core")
    in_specs = (
        P(None, "ctx", None, None, ch),
        P(None, None, ch),
        P(None, "ctx", None, ch),
        P(ch),
        P(ch, None),
    )
    return jax.shard_map(
        local, mesh=split, in_specs=in_specs, out_specs=P(None, "ctx", None, ch), check_vma=False
    )
```

```python
import math

import jax
import jax.numpy as jnp
import numpy as np
from jax import lax
from jax.experimental import pallas as pl
from jax.experimental.pallas import tpu as pltpu
from jax.sharding import Mesh, PartitionSpec as P

INTERPRET = False
MIB = 2**20
CTX_FIRST = 11
CHIP_FIRST = 14
LANES = 128
PERIOD = 2 * LANES


def in_hbm(value):
    return pltpu.with_memory_space_constraint(value, pltpu.HBM)


def tables():
    t = np.arange(LANES)[:, None]
    k = np.arange(LANES)[None, :]
    angle = 2.0 * math.pi * ((t * k) % PERIOD) / PERIOD
    sign = np.where(t % 2 == 0, 1.0, -1.0)
    cosine, sine = np.cos(angle), -np.sin(angle)
    forward = np.concatenate([cosine, np.where(k == 0, sign, sine)], axis=1)
    scale = np.where(k == 0, 1.0, 2.0) / PERIOD
    inverse = np.concatenate(
        [cosine * scale, np.where(k == 0, sign / PERIOD, sine * scale)], axis=1
    ).T

    def split(table, axis):
        high = table.astype(jnp.bfloat16)
        low = (table - high.astype(np.float64)).astype(jnp.bfloat16)
        return np.concatenate([high, low], axis=axis)

    return split(forward, 0), split(inverse, 1)


def pack_kernel(
    index_ref, features_hbm, filter_hbm, taps_hbm, gain_hbm, out_hbm, weights_ref, query_ref,
    features_ref, filter_ref, taps_ref, gain_ref, extended, edges, rows, turned, packed, sems, out_sems,
):
    groups = out_hbm.shape[0]
    channels = LANES // groups
    streams = features_ref.shape[1]
    taps = taps_ref.shape[1]
    rim = taps - 1
    copies = [
        pltpu.make_async_copy(taps_hbm, taps_ref, sems.at[3]),
        pltpu.make_async_copy(features_hbm.at[0], features_ref.at[0], sems.at[0]),
        pltpu.make_async_copy(features_hbm.at[1], features_ref.at[1], sems.at[1]),
        pltpu.make_async_copy(filter_hbm, filter_ref, sems.at[2]),
        pltpu.make_async_copy(gain_hbm, gain_ref, sems.at[4]),
    ]
    for copy in copies:
        copy.start()

    sent = []

    def put(row, tile):
        packed[row] = tile.T.astype(jnp.bfloat16).reshape(groups, channels, LANES)
        copy = pltpu.make_async_copy(packed.at[row], out_hbm.at[:, row], out_sems.at[row])
        copy.start()
        sent.append(copy)

    extended[:, :8] = jnp.zeros((streams, 8, LANES), jnp.float32)
    edges[...] = jnp.zeros_like(edges)
    rows[...] = jnp.zeros_like(rows)
    copies[0].wait()
    for half in range(2):
        copies[1 + half].wait()
        featured = []
        for stream in range(streams):
            value = features_ref[half, stream].astype(jnp.float32)
            extended[stream, 8:] = value
            base = 2 * rim * (half * streams + stream)
            edges[base : base + rim] = extended[stream, 8 + LANES - rim : 8 + LANES]
            edges[base + rim : base + 2 * rim] = extended[stream, 8 : 8 + rim]
            summed = taps_ref[stream, 0:1].astype(jnp.float32) * value
            for i in range(1, taps):
                weight = taps_ref[stream, i : i + 1].astype(jnp.float32)
                summed = summed + weight * extended[stream, 8 - i : 8 - i + LANES]
            featured.append(summed)
        query_ref[half] = featured[0]
        put(half, featured[1] * featured[2])
    copies[3].wait()
    for half in range(2):
        put(2 + half, filter_ref[half].astype(jnp.float32))
    put(4, edges[...])
    copies[4].wait()
    for stream in range(streams):
        rows[stream * 8 : stream * 8 + taps] = taps_ref[stream].astype(jnp.float32)
    rows[streams * 8 : streams * 8 + 1] = gain_ref[...]
    turned[...] = rows[...].T
    first = pl.multiple_of(index_ref[0] * channels, channels)
    weights_ref[...] = turned[pl.ds(first, channels)]
    for copy in sent:
        copy.wait()


def mix_kernel(
    packed_ref, weights_ref, forward_hbm, inverse_hbm, out_ref,
    query, keys, lags, key_spec, lag_spec, resp, total, forward_ref, inverse_ref, sems,
):
    forward_copy = pltpu.make_async_copy(forward_hbm, forward_ref, sems.at[0])
    inverse_copy = pltpu.make_async_copy(inverse_hbm, inverse_ref, sems.at[1])
    forward_copy.start()
    inverse_copy.start()
    pairs = packed_ref.shape[0]
    blocks = 2 * pairs
    channels = packed_ref.shape[2]
    streams, taps = 3, 7
    rim = taps - 1
    step = 2 * rim
    lane = lax.broadcasted_iota(jnp.int32, (channels, LANES), 1)

    def place(block):
        owner, half = (block, 0) if block < pairs else (blocks - 1 - block, 1)
        return (owner - CTX_FIRST) % pairs, half

    def span(block):
        return slice(block * channels, (block + 1) * channels)

    def column(index):
        return jnp.broadcast_to(weights_ref[:, index : index + 1], (channels, LANES))

    for block in range(blocks):
        source, half = place(block)
        lags[span(block)] = packed_ref[source, 2 + half]
    stream_of = lane // step % streams
    weight = [
        jnp.where(stream_of == 0, column(i), jnp.where(stream_of == 1, column(8 + i), column(16 + i)))
        for i in range(taps)
    ]
    tail = lane % step < rim
    lower = lane < streams * step
    edge = [packed_ref[place(owner)[0], 4].astype(jnp.float32) for owner in range(pairs)]
    head = lane < rim
    for owner in range(pairs):
        before = edge[owner - 1] if owner else jnp.zeros_like(edge[0])
        if owner + 1 < pairs:
            after = edge[owner + 1]
        else:
            after = pltpu.roll(edge[owner], streams * step, 1)
        value = jnp.where(tail, jnp.where(lower, before, after), edge[owner])
        summed = weight[0] * value
        for i in range(1, taps):
            summed = summed + weight[i] * pltpu.roll(value, i, 1)
        product = summed * pltpu.roll(summed, LANES - step, 1)
        for half, block in ((0, owner), (1, blocks - 1 - owner)):
            first = half * streams * step + rim
            gated = pltpu.roll(product, LANES - first - step, 1)
            whole = packed_ref[place(owner)[0], half].astype(jnp.float32)
            keys[span(block)] = jnp.where(head, gated, whole).astype(jnp.bfloat16)
            query[span(block)] = pltpu.roll(summed, LANES - first, 1)

    def transform(values):
        return jnp.dot(
            jnp.concatenate([values, values], axis=1), forward_ref[...], preferred_element_type=jnp.float32
        )

    forward_copy.wait()
    key_spec[...] = transform(keys[...])
    lag_spec[...] = transform(lags[...])
    parity = jnp.where(lane % 2 == 0, 1.0, -1.0).astype(jnp.float32)
    for block in range(blocks):
        real = lag_spec[span(block), :LANES]
        imag = lag_spec[span(block), LANES:]
        if block:
            real = real + parity * lag_spec[span(block - 1), :LANES]
            imag = imag + parity * lag_spec[span(block - 1), LANES:]
        cross = jnp.where(lane == 0, 0.0, imag)
        resp[0, span(block)] = real + cross
        resp[1, span(block)] = cross
        resp[2, span(block)] = jnp.where(lane == 0, imag, real) - cross
    group = 4
    for base in range(0, blocks, group):
        sums = [None] * group
        held = {}
        for block in range(base + group):
            real = key_spec[span(block), :LANES]
            imag = key_spec[span(block), LANES:]
            both = real + imag
            for j in range(group):
                gap = base + j - block
                if gap < 0:
                    continue
                if gap not in held:
                    held[gap] = [resp[i, span(gap)] for i in range(3)]
                terms = [one * other for one, other in zip((real, both, imag), held[gap])]
                if sums[j] is not None:
                    terms = [one + other for one, other in zip(sums[j], terms)]
                sums[j] = terms
        for j in range(group):
            total[span(base + j), :LANES] = sums[j][0] - sums[j][1]
            total[span(base + j), LANES:] = sums[j][1] + sums[j][2]
    inverse_copy.wait()
    high = total[...].astype(jnp.bfloat16)
    low = (total[...] - high.astype(jnp.float32)).astype(jnp.bfloat16)
    wide = jnp.dot(high, inverse_ref[...], preferred_element_type=jnp.float32)
    narrow = jnp.dot(low, inverse_ref[:, :LANES], preferred_element_type=jnp.float32)
    total[:, :LANES] = wide[:, :LANES] + (wide[:, LANES:] + narrow)
    gain = column(24)
    for block in range(blocks):
        target, half = place(block)
        inner = total[span(block), :LANES] + gain * keys[span(block)].astype(jnp.float32)
        out_ref[target, half] = jnp.where(head, query[span(block)] * inner, inner).astype(jnp.bfloat16)


def activate_kernel(mixed_ref, query_ref, out_ref):
    groups, halves, channels, length = mixed_ref.shape
    rim = 6
    token = lax.broadcasted_iota(jnp.int32, (length, LANES), 0)
    for half in range(halves):
        inner = mixed_ref[:, half].reshape(groups * channels, length).astype(jnp.float32).T
        product = jnp.where(token < rim, inner, query_ref[half] * inner)
        out_ref[half * length : (half + 1) * length] = product.astype(jnp.bfloat16)


def regroup_kernel(index_ref, own_hbm, other_hbm, out_ref, sems):
    chips = out_ref.shape[0] * out_ref.shape[2] // LANES
    step = chips // out_ref.shape[0]
    depth = own_hbm.shape[0]
    copies = []
    for chip in range(chips):
        block = 2 * ((chip + CHIP_FIRST) % chips) + index_ref[1]
        source = pl.ds(pl.multiple_of(block * LANES, LANES), LANES)
        columns = slice(chip % step * LANES, (chip % step + 1) * LANES)
        for i, weight in enumerate((own_hbm, other_hbm)):
            target = out_ref.at[chip // step, i * depth : (i + 1) * depth, columns]
            copies.append(pltpu.make_async_copy(weight.at[:, source], target, sems.at[i, chip]))
    for copy in copies:
        copy.start()
    for copy in copies:
        copy.wait()


def project_kernel(index_ref, both_ref, weight_ref, out_ref):
    width = out_ref.shape[2]
    core = index_ref[1]
    lhs = jnp.concatenate([both_ref[core], both_ref[1 - core]], axis=1)
    step = weight_ref.shape[2] // width
    for group in range(weight_ref.shape[0]):
        product = jnp.dot(lhs, weight_ref[group], preferred_element_type=jnp.float32).astype(jnp.bfloat16)
        for i in range(step):
            out_ref[group * step + i] = product[:, i * width : (i + 1) * width]


def local(features, short_weight, long_filter, skip_gain, out_weight):
    pairs = lax.axis_size("ctx")
    chips = lax.axis_size("chip")
    length = features.shape[2]
    width = features.shape[4]
    channels = width // pairs
    order = [[(place + CTX_FIRST) % pairs for place in range(pairs)]]
    chip_order = [[(place + CHIP_FIRST) % chips for place in range(chips)]]
    position = (lax.axis_index("ctx") + pairs - CTX_FIRST) % pairs
    index = jnp.stack([position, lax.axis_index("core")]).astype(jnp.int32)
    tiles = jnp.transpose(features, (0, 1, 3, 2, 4)).reshape(2, 3, length, width)
    taps = jnp.transpose(short_weight, (1, 0, 2))
    scalars = pl.BlockSpec(memory_space=pltpu.SMEM)
    vmem = pl.BlockSpec(memory_space=pltpu.VMEM)
    hbm = pl.BlockSpec(memory_space=pltpu.HBM)
    packed, weights, query = pl.pallas_call(
        pack_kernel,
        out_shape=(
            pltpu.HBM((pairs, 5, channels, length), jnp.bfloat16),
            pltpu.VMEM((channels, LANES), jnp.float32),
            pltpu.VMEM((2, length, width), jnp.float32),
        ),
        in_specs=[scalars] + [hbm] * 4,
        out_specs=(hbm, vmem, vmem),
        scratch_shapes=[
            pltpu.VMEM((2, 3, length, width), jnp.bfloat16),
            pltpu.VMEM((2, length, width), jnp.bfloat16),
            pltpu.VMEM(taps.shape, jnp.bfloat16),
            pltpu.VMEM((1, width), jnp.float32),
            pltpu.VMEM((3, 8 + length, width), jnp.float32),
            pltpu.VMEM((LANES, LANES), jnp.float32),
            pltpu.VMEM((LANES, LANES), jnp.float32),
            pltpu.VMEM((LANES, LANES), jnp.float32),
            pltpu.VMEM((5, pairs, channels, length), jnp.bfloat16),
            pltpu.SemaphoreType.DMA((5,)),
            pltpu.SemaphoreType.DMA((5,)),
        ],
        compiler_params=pltpu.CompilerParams(vmem_limit_bytes=4 * MIB),
        cost_estimate=pl.CostEstimate(flops=1000000, bytes_accessed=600000, transcendentals=0),
        interpret=INTERPRET,
    )(
        index,
        in_hbm(tiles),
        in_hbm(long_filter.reshape(2, length, width)),
        in_hbm(taps),
        in_hbm(skip_gain.reshape(1, width)),
    )
    packed = lax.all_to_all(packed, "ctx", 0, 0, tiled=True, axis_index_groups=order)
    other_weight = lax.ppermute(out_weight, "core", [(0, 1), (1, 0)])
    step = math.gcd(chips, 2)
    columns = pl.pallas_call(
        regroup_kernel,
        out_shape=pltpu.VMEM((chips // step, 2 * width, step * width), jnp.bfloat16),
        in_specs=[scalars, hbm, pl.BlockSpec(memory_space=pl.ANY)],
        out_specs=vmem,
        scratch_shapes=[pltpu.SemaphoreType.DMA((2, chips))],
        compiler_params=pltpu.CompilerParams(vmem_limit_bytes=4 * MIB),
        cost_estimate=pl.CostEstimate(flops=0, bytes_accessed=2 * MIB, transcendentals=0),
        interpret=INTERPRET,
    )(index, in_hbm(out_weight), other_weight)
    forward, inverse = tables()
    rows = 2 * pairs * channels
    mixed = pl.pallas_call(
        mix_kernel,
        out_shape=pltpu.VMEM((pairs, 2, channels, length), jnp.bfloat16),
        in_specs=[vmem] * 2 + [hbm] * 2,
        out_specs=vmem,
        scratch_shapes=[
            pltpu.VMEM((rows, LANES), jnp.float32),
            pltpu.VMEM((rows, LANES), jnp.bfloat16),
            pltpu.VMEM((rows, LANES), jnp.bfloat16),
            pltpu.VMEM((rows, PERIOD), jnp.float32),
            pltpu.VMEM((rows, PERIOD), jnp.float32),
            pltpu.VMEM((3, rows, LANES), jnp.float32),
            pltpu.VMEM((rows, PERIOD), jnp.float32),
            pltpu.VMEM(forward.shape, jnp.bfloat16),
            pltpu.VMEM(inverse.shape, jnp.bfloat16),
            pltpu.SemaphoreType.DMA((2,)),
        ],
        compiler_params=pltpu.CompilerParams(vmem_limit_bytes=6 * MIB),
        cost_estimate=pl.CostEstimate(flops=100000000, bytes_accessed=600000, transcendentals=0),
        interpret=INTERPRET,
    )(
        packed,
        weights,
        in_hbm(jnp.asarray(forward)),
        in_hbm(jnp.asarray(inverse)),
    )
    mixed = lax.all_to_all(mixed, "ctx", 0, 0, tiled=True, axis_index_groups=order)
    activated = pl.pallas_call(
        activate_kernel,
        out_shape=pltpu.VMEM((2 * length, width), jnp.bfloat16),
        in_specs=[vmem] * 2,
        out_specs=vmem,
        compiler_params=pltpu.CompilerParams(vmem_limit_bytes=4 * MIB),
        cost_estimate=pl.CostEstimate(flops=1000000, bytes_accessed=300000, transcendentals=0),
        interpret=INTERPRET,
    )(mixed, query)
    both = lax.all_gather(activated, "core", axis=0)
    partial = pl.pallas_call(
        project_kernel,
        out_shape=pltpu.VMEM((chips, 2 * length, width), jnp.bfloat16),
        in_specs=[scalars] + [vmem] * 2,
        out_specs=vmem,
        compiler_params=pltpu.CompilerParams(vmem_limit_bytes=8 * MIB),
        cost_estimate=pl.CostEstimate(flops=268435456, bytes_accessed=3300000, transcendentals=0),
        interpret=INTERPRET,
    )(index, both, columns)
    shares = lax.all_to_all(partial, "chip", 0, 0, tiled=True, axis_index_groups=chip_order)
    result = jnp.sum(shares.astype(jnp.float32), axis=0).astype(jnp.bfloat16)
    return result.reshape(2, 1, length, width)


def solution(mesh):
    pairs, parts = mesh.shape["ctx"], mesh.shape["ch"]
    split = Mesh(mesh.devices.reshape(pairs, parts // 2, 2), ("ctx", "chip", "core"))
    ch = ("chip", "core")
    in_specs = (
        P(None, "ctx", None, None, ch),
        P(None, None, ch),
        P(None, "ctx", None, ch),
        P(ch),
        P(ch, None),
    )
    return jax.shard_map(
        local, mesh=split, in_specs=in_specs, out_specs=P(None, "ctx", None, ch), check_vma=False
    )
```

```python
import math

import jax
import jax.numpy as jnp
import numpy as np
from jax import lax
from jax.experimental import pallas as pl
from jax.experimental.pallas import tpu as pltpu
from jax.sharding import Mesh, PartitionSpec as P

INTERPRET = False
MIB = 2**20
CTX_FIRST = 11
CHIP_FIRST = 14
LANES = 128
PERIOD = 2 * LANES


def in_hbm(value):
    return pltpu.with_memory_space_constraint(value, pltpu.HBM)


def tables():
    t = np.arange(LANES)[:, None]
    k = np.arange(LANES)[None, :]
    angle = 2.0 * math.pi * ((t * k) % PERIOD) / PERIOD
    sign = np.where(t % 2 == 0, 1.0, -1.0)
    cosine, sine = np.cos(angle), -np.sin(angle)
    forward = np.concatenate([cosine, np.where(k == 0, sign, sine)], axis=1)
    scale = np.where(k == 0, 1.0, 2.0) / PERIOD
    inverse = np.concatenate(
        [cosine * scale, np.where(k == 0, sign / PERIOD, sine * scale)], axis=1
    ).T

    def split(table, axis):
        high = table.astype(jnp.bfloat16)
        low = (table - high.astype(np.float64)).astype(jnp.bfloat16)
        return np.concatenate([high, low], axis=axis)

    return split(forward, 0), split(inverse, 1)


def pack_kernel(
    features_hbm, filter_hbm, taps_hbm, gain_hbm, out_hbm, weights_ref, query_ref,
    features_ref, filter_ref, taps_ref, gain_ref, extended, edges, rows, turned, packed, sems, out_sems,
):
    groups = out_hbm.shape[0]
    channels = LANES // groups
    streams = features_ref.shape[1]
    taps = taps_ref.shape[1]
    rim = taps - 1
    copies = [
        pltpu.make_async_copy(taps_hbm, taps_ref, sems.at[3]),
        pltpu.make_async_copy(features_hbm.at[0], features_ref.at[0], sems.at[0]),
        pltpu.make_async_copy(features_hbm.at[1], features_ref.at[1], sems.at[1]),
        pltpu.make_async_copy(filter_hbm, filter_ref, sems.at[2]),
        pltpu.make_async_copy(gain_hbm, gain_ref, sems.at[4]),
    ]
    for copy in copies:
        copy.start()

    sent = []

    def put(row, tile):
        packed[row] = tile.T.astype(jnp.bfloat16).reshape(groups, channels, LANES)
        copy = pltpu.make_async_copy(packed.at[row], out_hbm.at[:, row], out_sems.at[row])
        copy.start()
        sent.append(copy)

    extended[:, :8] = jnp.zeros((streams, 8, LANES), jnp.float32)
    edges[...] = jnp.zeros_like(edges)
    rows[...] = jnp.zeros_like(rows)
    copies[0].wait()
    for half in range(2):
        copies[1 + half].wait()
        featured = []
        for stream in range(streams):
            value = features_ref[half, stream].astype(jnp.float32)
            extended[stream, 8:] = value
            base = 2 * rim * (half * streams + stream)
            edges[base : base + rim] = extended[stream, 8 + LANES - rim : 8 + LANES]
            edges[base + rim : base + 2 * rim] = extended[stream, 8 : 8 + rim]
            summed = taps_ref[stream, 0:1].astype(jnp.float32) * value
            for i in range(1, taps):
                weight = taps_ref[stream, i : i + 1].astype(jnp.float32)
                summed = summed + weight * extended[stream, 8 - i : 8 - i + LANES]
            featured.append(summed)
        query_ref[half] = featured[0]
        put(half, featured[1] * featured[2])
    copies[3].wait()
    for half in range(2):
        put(2 + half, filter_ref[half].astype(jnp.float32))
    put(4, edges[...])
    copies[4].wait()
    for stream in range(streams):
        rows[stream * 8 : stream * 8 + taps] = taps_ref[stream].astype(jnp.float32)
    rows[streams * 8 : streams * 8 + 1] = gain_ref[...]
    turned[...] = rows[...].T
    position = (lax.axis_index("ctx") + groups - CTX_FIRST) % groups
    first = pl.multiple_of(position * channels, channels)
    weights_ref[...] = turned[pl.ds(first, channels)]
    for copy in sent:
        copy.wait()


def mix_kernel(
    packed_ref, weights_ref, forward_ref, inverse_ref, out_ref,
    query, keys, lags, key_spec, lag_spec, resp, total,
):
    pairs = packed_ref.shape[0]
    blocks = 2 * pairs
    channels = packed_ref.shape[2]
    streams, taps = 3, 7
    rim = taps - 1
    step = 2 * rim
    lane = lax.broadcasted_iota(jnp.int32, (channels, LANES), 1)

    def place(block):
        owner, half = (block, 0) if block < pairs else (blocks - 1 - block, 1)
        return (owner - CTX_FIRST) % pairs, half

    def span(block):
        return slice(block * channels, (block + 1) * channels)

    def column(index):
        return jnp.broadcast_to(weights_ref[:, index : index + 1], (channels, LANES))

    for block in range(blocks):
        source, half = place(block)
        lags[span(block)] = packed_ref[source, 2 + half]
    stream_of = lane // step % streams
    weight = [
        jnp.where(stream_of == 0, column(i), jnp.where(stream_of == 1, column(8 + i), column(16 + i)))
        for i in range(taps)
    ]
    tail = lane % step < rim
    lower = lane < streams * step
    edge = [packed_ref[place(owner)[0], 4].astype(jnp.float32) for owner in range(pairs)]
    head = lane < rim
    for owner in range(pairs):
        before = edge[owner - 1] if owner else jnp.zeros_like(edge[0])
        if owner + 1 < pairs:
            after = edge[owner + 1]
        else:
            after = pltpu.roll(edge[owner], streams * step, 1)
        value = jnp.where(tail, jnp.where(lower, before, after), edge[owner])
        summed = weight[0] * value
        for i in range(1, taps):
            summed = summed + weight[i] * pltpu.roll(value, i, 1)
        product = summed * pltpu.roll(summed, LANES - step, 1)
        for half, block in ((0, owner), (1, blocks - 1 - owner)):
            first = half * streams * step + rim
            gated = pltpu.roll(product, LANES - first - step, 1)
            whole = packed_ref[place(owner)[0], half].astype(jnp.float32)
            keys[span(block)] = jnp.where(head, gated, whole).astype(jnp.bfloat16)
            query[span(block)] = pltpu.roll(summed, LANES - first, 1)

    def transform(values):
        return jnp.dot(
            jnp.concatenate([values, values], axis=1), forward_ref[...], preferred_element_type=jnp.float32
        )

    key_spec[...] = transform(keys[...])
    lag_spec[...] = transform(lags[...])
    parity = jnp.where(lane % 2 == 0, 1.0, -1.0).astype(jnp.float32)
    for block in range(blocks):
        real = lag_spec[span(block), :LANES]
        imag = lag_spec[span(block), LANES:]
        if block:
            real = real + parity * lag_spec[span(block - 1), :LANES]
            imag = imag + parity * lag_spec[span(block - 1), LANES:]
        cross = jnp.where(lane == 0, 0.0, imag)
        resp[0, span(block)] = real + cross
        resp[1, span(block)] = cross
        resp[2, span(block)] = jnp.where(lane == 0, imag, real) - cross
    group = 4
    for base in range(0, blocks, group):
        sums = [None] * group
        held = {}
        for block in range(base + group):
            real = key_spec[span(block), :LANES]
            imag = key_spec[span(block), LANES:]
            both = real + imag
            for j in range(group):
                gap = base + j - block
                if gap < 0:
                    continue
                if gap not in held:
                    held[gap] = [resp[i, span(gap)] for i in range(3)]
                terms = [one * other for one, other in zip((real, both, imag), held[gap])]
                if sums[j] is not None:
                    terms = [one + other for one, other in zip(sums[j], terms)]
                sums[j] = terms
        for j in range(group):
            total[span(base + j), :LANES] = sums[j][0] - sums[j][1]
            total[span(base + j), LANES:] = sums[j][1] + sums[j][2]
    high = total[...].astype(jnp.bfloat16)
    low = (total[...] - high.astype(jnp.float32)).astype(jnp.bfloat16)
    wide = jnp.dot(high, inverse_ref[...], preferred_element_type=jnp.float32)
    narrow = jnp.dot(low, inverse_ref[:, :LANES], preferred_element_type=jnp.float32)
    total[:, :LANES] = wide[:, :LANES] + (wide[:, LANES:] + narrow)
    gain = column(24)
    for block in range(blocks):
        target, half = place(block)
        inner = total[span(block), :LANES] + gain * keys[span(block)].astype(jnp.float32)
        out_ref[target, half] = jnp.where(head, query[span(block)] * inner, inner).astype(jnp.bfloat16)


def activate_kernel(mixed_ref, query_ref, out_ref):
    groups, halves, channels, length = mixed_ref.shape
    rim = 6
    token = lax.broadcasted_iota(jnp.int32, (length, LANES), 0)
    for half in range(halves):
        inner = mixed_ref[:, half].reshape(groups * channels, length).astype(jnp.float32).T
        product = jnp.where(token < rim, inner, query_ref[half] * inner)
        out_ref[half * length : (half + 1) * length] = product.astype(jnp.bfloat16)


def regroup_kernel(
    own_hbm, other_hbm, forward_hbm, inverse_hbm, out_ref, forward_ref, inverse_ref, sems, table_sems
):
    chips = out_ref.shape[0] * out_ref.shape[2] // LANES
    step = chips // out_ref.shape[0]
    depth = own_hbm.shape[0]
    core = lax.axis_index("core")
    copies = [
        pltpu.make_async_copy(forward_hbm, forward_ref, table_sems.at[0]),
        pltpu.make_async_copy(inverse_hbm, inverse_ref, table_sems.at[1]),
    ]
    for chip in range(chips):
        block = 2 * ((chip + CHIP_FIRST) % chips) + core
        source = pl.ds(pl.multiple_of(block * LANES, LANES), LANES)
        columns = slice(chip % step * LANES, (chip % step + 1) * LANES)
        for i, weight in enumerate((own_hbm, other_hbm)):
            rows = pl.ds(pl.multiple_of((core + i) % 2 * depth, depth), depth)
            target = out_ref.at[chip // step, rows, columns]
            copies.append(pltpu.make_async_copy(weight.at[:, source], target, sems.at[i, chip]))
    for copy in copies:
        copy.start()
    for copy in copies:
        copy.wait()


def project_kernel(both_ref, weight_ref, out_ref):
    width = out_ref.shape[2]
    lhs = jnp.concatenate([both_ref[0], both_ref[1]], axis=1)
    step = weight_ref.shape[2] // width
    for group in range(weight_ref.shape[0]):
        product = jnp.dot(lhs, weight_ref[group], preferred_element_type=jnp.float32).astype(jnp.bfloat16)
        for i in range(step):
            out_ref[group * step + i] = product[:, i * width : (i + 1) * width]


def local(features, short_weight, long_filter, skip_gain, out_weight):
    pairs = lax.axis_size("ctx")
    chips = lax.axis_size("chip")
    length = features.shape[2]
    width = features.shape[4]
    channels = width // pairs
    order = [[(place + CTX_FIRST) % pairs for place in range(pairs)]]
    chip_order = [[(place + CHIP_FIRST) % chips for place in range(chips)]]
    tiles = jnp.transpose(features, (0, 1, 3, 2, 4)).reshape(2, 3, length, width)
    taps = jnp.transpose(short_weight, (1, 0, 2))
    vmem = pl.BlockSpec(memory_space=pltpu.VMEM)
    hbm = pl.BlockSpec(memory_space=pltpu.HBM)
    packed, weights, query = pl.pallas_call(
        pack_kernel,
        out_shape=(
            pltpu.HBM((pairs, 5, channels, length), jnp.bfloat16),
            pltpu.VMEM((channels, LANES), jnp.float32),
            pltpu.VMEM((2, length, width), jnp.float32),
        ),
        in_specs=[hbm] * 4,
        out_specs=(hbm, vmem, vmem),
        scratch_shapes=[
            pltpu.VMEM((2, 3, length, width), jnp.bfloat16),
            pltpu.VMEM((2, length, width), jnp.bfloat16),
            pltpu.VMEM(taps.shape, jnp.bfloat16),
            pltpu.VMEM((1, width), jnp.float32),
            pltpu.VMEM((3, 8 + length, width), jnp.float32),
            pltpu.VMEM((LANES, LANES), jnp.float32),
            pltpu.VMEM((LANES, LANES), jnp.float32),
            pltpu.VMEM((LANES, LANES), jnp.float32),
            pltpu.VMEM((5, pairs, channels, length), jnp.bfloat16),
            pltpu.SemaphoreType.DMA((5,)),
            pltpu.SemaphoreType.DMA((5,)),
        ],
        compiler_params=pltpu.CompilerParams(vmem_limit_bytes=4 * MIB),
        cost_estimate=pl.CostEstimate(flops=1000000, bytes_accessed=600000, transcendentals=0),
        interpret=INTERPRET,
    )(
        in_hbm(tiles),
        in_hbm(long_filter.reshape(2, length, width)),
        in_hbm(taps),
        in_hbm(skip_gain.reshape(1, width)),
    )
    packed = lax.all_to_all(packed, "ctx", 0, 0, tiled=True, axis_index_groups=order)
    other_weight = lax.ppermute(out_weight, "core", [(0, 1), (1, 0)])
    step = math.gcd(chips, 2)
    forward, inverse = tables()
    columns, forward, inverse = pl.pallas_call(
        regroup_kernel,
        out_shape=(
            pltpu.VMEM((chips // step, 2 * width, step * width), jnp.bfloat16),
            pltpu.VMEM(forward.shape, jnp.bfloat16),
            pltpu.VMEM(inverse.shape, jnp.bfloat16),
        ),
        in_specs=[hbm, pl.BlockSpec(memory_space=pl.ANY), hbm, hbm],
        out_specs=(vmem, vmem, vmem),
        scratch_shapes=[pltpu.SemaphoreType.DMA((2, chips)), pltpu.SemaphoreType.DMA((2,))],
        compiler_params=pltpu.CompilerParams(vmem_limit_bytes=4 * MIB),
        cost_estimate=pl.CostEstimate(flops=0, bytes_accessed=2 * MIB, transcendentals=0),
        interpret=INTERPRET,
    )(in_hbm(out_weight), other_weight, in_hbm(jnp.asarray(forward)), in_hbm(jnp.asarray(inverse)))
    rows = 2 * pairs * channels
    mixed = pl.pallas_call(
        mix_kernel,
        out_shape=pltpu.VMEM((pairs, 2, channels, length), jnp.bfloat16),
        in_specs=[vmem] * 4,
        out_specs=vmem,
        scratch_shapes=[
            pltpu.VMEM((rows, LANES), jnp.float32),
            pltpu.VMEM((rows, LANES), jnp.bfloat16),
            pltpu.VMEM((rows, LANES), jnp.bfloat16),
            pltpu.VMEM((rows, PERIOD), jnp.float32),
            pltpu.VMEM((rows, PERIOD), jnp.float32),
            pltpu.VMEM((3, rows, LANES), jnp.float32),
            pltpu.VMEM((rows, PERIOD), jnp.float32),
        ],
        compiler_params=pltpu.CompilerParams(vmem_limit_bytes=6 * MIB),
        cost_estimate=pl.CostEstimate(flops=100000000, bytes_accessed=600000, transcendentals=0),
        interpret=INTERPRET,
    )(
        packed,
        weights,
        forward,
        inverse,
    )
    mixed = lax.all_to_all(mixed, "ctx", 0, 0, tiled=True, axis_index_groups=order)
    activated = pl.pallas_call(
        activate_kernel,
        out_shape=pltpu.VMEM((2 * length, width), jnp.bfloat16),
        in_specs=[vmem] * 2,
        out_specs=vmem,
        compiler_params=pltpu.CompilerParams(vmem_limit_bytes=4 * MIB),
        cost_estimate=pl.CostEstimate(flops=1000000, bytes_accessed=300000, transcendentals=0),
        interpret=INTERPRET,
    )(mixed, query)
    both = lax.all_gather(activated, "core", axis=0)
    partial = pl.pallas_call(
        project_kernel,
        out_shape=pltpu.VMEM((chips, 2 * length, width), jnp.bfloat16),
        in_specs=[vmem] * 2,
        out_specs=vmem,
        compiler_params=pltpu.CompilerParams(vmem_limit_bytes=8 * MIB),
        cost_estimate=pl.CostEstimate(flops=268435456, bytes_accessed=3300000, transcendentals=0),
        interpret=INTERPRET,
    )(both, columns)
    shares = lax.all_to_all(partial, "chip", 0, 0, tiled=True, axis_index_groups=chip_order)
    result = jnp.sum(shares.astype(jnp.float32), axis=0).astype(jnp.bfloat16)
    return result.reshape(2, 1, length, width)


def solution(mesh):
    pairs, parts = mesh.shape["ctx"], mesh.shape["ch"]
    split = Mesh(mesh.devices.reshape(pairs, parts // 2, 2), ("ctx", "chip", "core"))
    ch = ("chip", "core")
    in_specs = (
        P(None, "ctx", None, None, ch),
        P(None, None, ch),
        P(None, "ctx", None, ch),
        P(ch),
        P(ch, None),
    )
    return jax.shard_map(
        local, mesh=split, in_specs=in_specs, out_specs=P(None, "ctx", None, ch), check_vma=False
    )
```

```python
import math

import jax
import jax.numpy as jnp
import numpy as np
from jax import lax
from jax.experimental import pallas as pl
from jax.experimental.pallas import tpu as pltpu
from jax.sharding import Mesh, PartitionSpec as P

INTERPRET = False
MIB = 2**20
CTX_FIRST = 11
BACK_FIRST = 9
CHIP_FIRST = 10
LANES = 128
PERIOD = 2 * LANES


def in_hbm(value):
    return pltpu.with_memory_space_constraint(value, pltpu.HBM)


def tables():
    t = np.arange(LANES)[:, None]
    k = np.arange(LANES)[None, :]
    angle = 2.0 * math.pi * ((t * k) % PERIOD) / PERIOD
    sign = np.where(t % 2 == 0, 1.0, -1.0)
    cosine, sine = np.cos(angle), -np.sin(angle)
    forward = np.concatenate([cosine, np.where(k == 0, sign, sine)], axis=1)
    scale = np.where(k == 0, 1.0, 2.0) / PERIOD
    inverse = np.concatenate(
        [cosine * scale, np.where(k == 0, sign / PERIOD, sine * scale)], axis=1
    ).T

    def split(table, axis):
        high = table.astype(jnp.bfloat16)
        low = (table - high.astype(np.float64)).astype(jnp.bfloat16)
        return np.concatenate([high, low], axis=axis)

    return split(forward, 0), split(inverse, 1)


def pack_kernel(
    features_hbm, filter_hbm, taps_hbm, gain_hbm, out_hbm, weights_ref, query_ref,
    features_ref, filter_ref, taps_ref, gain_ref, extended, edges, rows, turned, packed, sems, out_sems,
):
    groups = out_hbm.shape[0]
    channels = LANES // groups
    streams = features_ref.shape[1]
    taps = taps_ref.shape[1]
    rim = taps - 1
    copies = [
        pltpu.make_async_copy(taps_hbm, taps_ref, sems.at[3]),
        pltpu.make_async_copy(features_hbm.at[0], features_ref.at[0], sems.at[0]),
        pltpu.make_async_copy(features_hbm.at[1], features_ref.at[1], sems.at[1]),
        pltpu.make_async_copy(filter_hbm, filter_ref, sems.at[2]),
        pltpu.make_async_copy(gain_hbm, gain_ref, sems.at[4]),
    ]
    for copy in copies:
        copy.start()

    sent = []

    def put(row, tile):
        packed[row] = tile.T.astype(jnp.bfloat16).reshape(groups, channels, LANES)
        copy = pltpu.make_async_copy(packed.at[row], out_hbm.at[:, row], out_sems.at[row])
        copy.start()
        sent.append(copy)

    extended[:, :8] = jnp.zeros((streams, 8, LANES), jnp.float32)
    edges[...] = jnp.zeros_like(edges)
    rows[...] = jnp.zeros_like(rows)
    copies[0].wait()
    for half in range(2):
        copies[1 + half].wait()
        featured = []
        for stream in range(streams):
            value = features_ref[half, stream].astype(jnp.float32)
            extended[stream, 8:] = value
            base = 2 * rim * (half * streams + stream)
            edges[base : base + rim] = extended[stream, 8 + LANES - rim : 8 + LANES]
            edges[base + rim : base + 2 * rim] = extended[stream, 8 : 8 + rim]
            summed = taps_ref[stream, 0:1].astype(jnp.float32) * value
            for i in range(1, taps):
                weight = taps_ref[stream, i : i + 1].astype(jnp.float32)
                summed = summed + weight * extended[stream, 8 - i : 8 - i + LANES]
            featured.append(summed)
        query_ref[half] = featured[0]
        put(half, featured[1] * featured[2])
    copies[3].wait()
    for half in range(2):
        put(2 + half, filter_ref[half].astype(jnp.float32))
    put(4, edges[...])
    copies[4].wait()
    for stream in range(streams):
        rows[stream * 8 : stream * 8 + taps] = taps_ref[stream].astype(jnp.float32)
    rows[streams * 8 : streams * 8 + 1] = gain_ref[...]
    turned[...] = rows[...].T
    position = (lax.axis_index("ctx") + groups - CTX_FIRST) % groups
    first = pl.multiple_of(position * channels, channels)
    weights_ref[...] = turned[pl.ds(first, channels)]
    for copy in sent:
        copy.wait()


def mix_kernel(
    packed_ref, weights_ref, forward_ref, inverse_ref, out_ref,
    query, keys, lags, key_spec, lag_spec, resp, total,
):
    pairs = packed_ref.shape[0]
    blocks = 2 * pairs
    channels = packed_ref.shape[2]
    streams, taps = 3, 7
    rim = taps - 1
    step = 2 * rim
    lane = lax.broadcasted_iota(jnp.int32, (channels, LANES), 1)

    def place(block):
        owner, half = (block, 0) if block < pairs else (blocks - 1 - block, 1)
        return (owner - CTX_FIRST) % pairs, half

    def span(block):
        return slice(block * channels, (block + 1) * channels)

    def column(index):
        return jnp.broadcast_to(weights_ref[:, index : index + 1], (channels, LANES))

    for block in range(blocks):
        source, half = place(block)
        lags[span(block)] = packed_ref[source, 2 + half]
    stream_of = lane // step % streams
    weight = [
        jnp.where(stream_of == 0, column(i), jnp.where(stream_of == 1, column(8 + i), column(16 + i)))
        for i in range(taps)
    ]
    tail = lane % step < rim
    lower = lane < streams * step
    edge = [packed_ref[place(owner)[0], 4].astype(jnp.float32) for owner in range(pairs)]
    head = lane < rim
    for owner in range(pairs):
        before = edge[owner - 1] if owner else jnp.zeros_like(edge[0])
        if owner + 1 < pairs:
            after = edge[owner + 1]
        else:
            after = pltpu.roll(edge[owner], streams * step, 1)
        value = jnp.where(tail, jnp.where(lower, before, after), edge[owner])
        summed = weight[0] * value
        for i in range(1, taps):
            summed = summed + weight[i] * pltpu.roll(value, i, 1)
        product = summed * pltpu.roll(summed, LANES - step, 1)
        for half, block in ((0, owner), (1, blocks - 1 - owner)):
            first = half * streams * step + rim
            gated = pltpu.roll(product, LANES - first - step, 1)
            whole = packed_ref[place(owner)[0], half].astype(jnp.float32)
            keys[span(block)] = jnp.where(head, gated, whole).astype(jnp.bfloat16)
            query[span(block)] = pltpu.roll(summed, LANES - first, 1)

    def transform(values):
        return jnp.dot(
            jnp.concatenate([values, values], axis=1), forward_ref[...], preferred_element_type=jnp.float32
        )

    key_spec[...] = transform(keys[...])
    lag_spec[...] = transform(lags[...])
    parity = jnp.where(lane % 2 == 0, 1.0, -1.0).astype(jnp.float32)
    for block in range(blocks):
        real = lag_spec[span(block), :LANES]
        imag = lag_spec[span(block), LANES:]
        if block:
            real = real + parity * lag_spec[span(block - 1), :LANES]
            imag = imag + parity * lag_spec[span(block - 1), LANES:]
        cross = jnp.where(lane == 0, 0.0, imag)
        resp[0, span(block)] = real + cross
        resp[1, span(block)] = cross
        resp[2, span(block)] = jnp.where(lane == 0, imag, real) - cross
    group = 4
    for base in range(0, blocks, group):
        sums = [None] * group
        held = {}
        for block in range(base + group):
            real = key_spec[span(block), :LANES]
            imag = key_spec[span(block), LANES:]
            both = real + imag
            for j in range(group):
                gap = base + j - block
                if gap < 0:
                    continue
                if gap not in held:
                    held[gap] = [resp[i, span(gap)] for i in range(3)]
                terms = [one * other for one, other in zip((real, both, imag), held[gap])]
                if sums[j] is not None:
                    terms = [one + other for one, other in zip(sums[j], terms)]
                sums[j] = terms
        for j in range(group):
            total[span(base + j), :LANES] = sums[j][0] - sums[j][1]
            total[span(base + j), LANES:] = sums[j][1] + sums[j][2]
    high = total[...].astype(jnp.bfloat16)
    low = (total[...] - high.astype(jnp.float32)).astype(jnp.bfloat16)
    wide = jnp.dot(high, inverse_ref[...], preferred_element_type=jnp.float32)
    narrow = jnp.dot(low, inverse_ref[:, :LANES], preferred_element_type=jnp.float32)
    total[:, :LANES] = wide[:, :LANES] + (wide[:, LANES:] + narrow)
    gain = column(24)
    for block in range(blocks):
        owner, half = (block, 0) if block < pairs else (blocks - 1 - block, 1)
        target = (owner - BACK_FIRST) % pairs
        inner = total[span(block), :LANES] + gain * keys[span(block)].astype(jnp.float32)
        out_ref[target, half] = jnp.where(head, query[span(block)] * inner, inner).astype(jnp.bfloat16)


def activate_kernel(mixed_ref, query_ref, out_ref):
    groups, halves, channels, length = mixed_ref.shape
    start = (CTX_FIRST - BACK_FIRST) % groups
    rim = 6
    token = lax.broadcasted_iota(jnp.int32, (length, LANES), 0)
    for half in range(halves):
        parts = [mixed_ref[start:, half], mixed_ref[:start, half]]
        inner = jnp.concatenate(parts, axis=0).reshape(groups * channels, length).astype(jnp.float32).T
        product = jnp.where(token < rim, inner, query_ref[half] * inner)
        out_ref[half * length : (half + 1) * length] = product.astype(jnp.bfloat16)


def regroup_kernel(
    own_hbm, other_hbm, forward_hbm, inverse_hbm, out_ref, forward_ref, inverse_ref, sems, table_sems
):
    chips = out_ref.shape[0] * out_ref.shape[2] // LANES
    step = chips // out_ref.shape[0]
    depth = own_hbm.shape[0]
    core = lax.axis_index("core")
    copies = [
        pltpu.make_async_copy(forward_hbm, forward_ref, table_sems.at[0]),
        pltpu.make_async_copy(inverse_hbm, inverse_ref, table_sems.at[1]),
    ]
    for chip in range(chips):
        block = 2 * ((chip + CHIP_FIRST) % chips) + core
        source = pl.ds(pl.multiple_of(block * LANES, LANES), LANES)
        columns = slice(chip % step * LANES, (chip % step + 1) * LANES)
        for i, weight in enumerate((own_hbm, other_hbm)):
            rows = pl.ds(pl.multiple_of((core + i) % 2 * depth, depth), depth)
            target = out_ref.at[chip // step, rows, columns]
            copies.append(pltpu.make_async_copy(weight.at[:, source], target, sems.at[i, chip]))
    for copy in copies:
        copy.start()
    for copy in copies:
        copy.wait()


def project_kernel(both_ref, weight_ref, out_ref):
    width = out_ref.shape[2]
    lhs = jnp.concatenate([both_ref[0], both_ref[1]], axis=1)
    step = weight_ref.shape[2] // width
    for group in range(weight_ref.shape[0]):
        product = jnp.dot(lhs, weight_ref[group], preferred_element_type=jnp.float32).astype(jnp.bfloat16)
        for i in range(step):
            out_ref[group * step + i] = product[:, i * width : (i + 1) * width]


def local(features, short_weight, long_filter, skip_gain, out_weight):
    pairs = lax.axis_size("ctx")
    chips = lax.axis_size("chip")
    length = features.shape[2]
    width = features.shape[4]
    channels = width // pairs
    order = [[(place + CTX_FIRST) % pairs for place in range(pairs)]]
    back_order = [[(place + BACK_FIRST) % pairs for place in range(pairs)]]
    chip_order = [[(place + CHIP_FIRST) % chips for place in range(chips)]]
    tiles = jnp.transpose(features, (0, 1, 3, 2, 4)).reshape(2, 3, length, width)
    taps = jnp.transpose(short_weight, (1, 0, 2))
    vmem = pl.BlockSpec(memory_space=pltpu.VMEM)
    hbm = pl.BlockSpec(memory_space=pltpu.HBM)
    packed, weights, query = pl.pallas_call(
        pack_kernel,
        out_shape=(
            pltpu.HBM((pairs, 5, channels, length), jnp.bfloat16),
            pltpu.VMEM((channels, LANES), jnp.float32),
            pltpu.VMEM((2, length, width), jnp.float32),
        ),
        in_specs=[hbm] * 4,
        out_specs=(hbm, vmem, vmem),
        scratch_shapes=[
            pltpu.VMEM((2, 3, length, width), jnp.bfloat16),
            pltpu.VMEM((2, length, width), jnp.bfloat16),
            pltpu.VMEM(taps.shape, jnp.bfloat16),
            pltpu.VMEM((1, width), jnp.float32),
            pltpu.VMEM((3, 8 + length, width), jnp.float32),
            pltpu.VMEM((LANES, LANES), jnp.float32),
            pltpu.VMEM((LANES, LANES), jnp.float32),
            pltpu.VMEM((LANES, LANES), jnp.float32),
            pltpu.VMEM((5, pairs, channels, length), jnp.bfloat16),
            pltpu.SemaphoreType.DMA((5,)),
            pltpu.SemaphoreType.DMA((5,)),
        ],
        compiler_params=pltpu.CompilerParams(vmem_limit_bytes=4 * MIB),
        cost_estimate=pl.CostEstimate(flops=1000000, bytes_accessed=600000, transcendentals=0),
        interpret=INTERPRET,
    )(
        in_hbm(tiles),
        in_hbm(long_filter.reshape(2, length, width)),
        in_hbm(taps),
        in_hbm(skip_gain.reshape(1, width)),
    )
    packed = lax.all_to_all(packed, "ctx", 0, 0, tiled=True, axis_index_groups=order)
    other_weight = lax.ppermute(out_weight, "core", [(0, 1), (1, 0)])
    step = math.gcd(chips, 2)
    forward, inverse = tables()
    columns, forward, inverse = pl.pallas_call(
        regroup_kernel,
        out_shape=(
            pltpu.VMEM((chips // step, 2 * width, step * width), jnp.bfloat16),
            pltpu.VMEM(forward.shape, jnp.bfloat16),
            pltpu.VMEM(inverse.shape, jnp.bfloat16),
        ),
        in_specs=[hbm, pl.BlockSpec(memory_space=pl.ANY), hbm, hbm],
        out_specs=(vmem, vmem, vmem),
        scratch_shapes=[pltpu.SemaphoreType.DMA((2, chips)), pltpu.SemaphoreType.DMA((2,))],
        compiler_params=pltpu.CompilerParams(vmem_limit_bytes=4 * MIB),
        cost_estimate=pl.CostEstimate(flops=0, bytes_accessed=2 * MIB, transcendentals=0),
        interpret=INTERPRET,
    )(
        in_hbm(out_weight),
        other_weight,
        in_hbm(jnp.asarray(forward)),
        in_hbm(jnp.asarray(inverse)),
    )
    rows = 2 * pairs * channels
    mixed = pl.pallas_call(
        mix_kernel,
        out_shape=pltpu.VMEM((pairs, 2, channels, length), jnp.bfloat16),
        in_specs=[vmem] * 4,
        out_specs=vmem,
        scratch_shapes=[
            pltpu.VMEM((rows, LANES), jnp.float32),
            pltpu.VMEM((rows, LANES), jnp.bfloat16),
            pltpu.VMEM((rows, LANES), jnp.bfloat16),
            pltpu.VMEM((rows, PERIOD), jnp.float32),
            pltpu.VMEM((rows, PERIOD), jnp.float32),
            pltpu.VMEM((3, rows, LANES), jnp.float32),
            pltpu.VMEM((rows, PERIOD), jnp.float32),
        ],
        compiler_params=pltpu.CompilerParams(vmem_limit_bytes=6 * MIB),
        cost_estimate=pl.CostEstimate(flops=100000000, bytes_accessed=600000, transcendentals=0),
        interpret=INTERPRET,
    )(
        packed,
        weights,
        forward,
        inverse,
    )
    mixed = lax.all_to_all(mixed, "ctx", 0, 0, tiled=True, axis_index_groups=back_order)
    activated = pl.pallas_call(
        activate_kernel,
        out_shape=pltpu.VMEM((2 * length, width), jnp.bfloat16),
        in_specs=[vmem] * 2,
        out_specs=vmem,
        compiler_params=pltpu.CompilerParams(vmem_limit_bytes=4 * MIB),
        cost_estimate=pl.CostEstimate(flops=1000000, bytes_accessed=300000, transcendentals=0),
        interpret=INTERPRET,
    )(mixed, query)
    both = lax.all_gather(activated, "core", axis=0)
    partial = pl.pallas_call(
        project_kernel,
        out_shape=pltpu.VMEM((chips, 2 * length, width), jnp.bfloat16),
        in_specs=[vmem] * 2,
        out_specs=vmem,
        compiler_params=pltpu.CompilerParams(vmem_limit_bytes=8 * MIB),
        cost_estimate=pl.CostEstimate(flops=268435456, bytes_accessed=3300000, transcendentals=0),
        interpret=INTERPRET,
    )(both, columns)
    shares = lax.all_to_all(partial, "chip", 0, 0, tiled=True, axis_index_groups=chip_order)
    result = jnp.sum(shares.astype(jnp.float32), axis=0).astype(jnp.bfloat16)
    return result.reshape(2, 1, length, width)


def solution(mesh):
    pairs, parts = mesh.shape["ctx"], mesh.shape["ch"]
    split = Mesh(mesh.devices.reshape(pairs, parts // 2, 2), ("ctx", "chip", "core"))
    ch = ("chip", "core")
    in_specs = (
        P(None, "ctx", None, None, ch),
        P(None, None, ch),
        P(None, "ctx", None, ch),
        P(ch),
        P(ch, None),
    )
    return jax.shard_map(local, mesh=split, in_specs=in_specs, out_specs=P(None, "ctx", None, ch), check_vma=False)
```

```python
import math

import jax
import jax.numpy as jnp
import numpy as np
from jax import lax
from jax.experimental import pallas as pl
from jax.experimental.pallas import tpu as pltpu
from jax.sharding import Mesh, PartitionSpec as P

INTERPRET = False
MIB = 2**20
CTX_FIRST = 11
BACK_FIRST = 8
CHIP_FIRST = 14
LANES = 128
PERIOD = 2 * LANES


def in_hbm(value):
    return pltpu.with_memory_space_constraint(value, pltpu.HBM)


def tables():
    t = np.arange(LANES)[:, None]
    k = np.arange(LANES)[None, :]
    angle = 2.0 * math.pi * ((t * k) % PERIOD) / PERIOD
    sign = np.where(t % 2 == 0, 1.0, -1.0)
    cosine, sine = np.cos(angle), -np.sin(angle)
    forward = np.concatenate([cosine, np.where(k == 0, sign, sine)], axis=1)
    scale = np.where(k == 0, 1.0, 2.0) / PERIOD
    inverse = np.concatenate(
        [cosine * scale, np.where(k == 0, sign / PERIOD, sine * scale)], axis=1
    ).T

    def split(table, axis):
        high = table.astype(jnp.bfloat16)
        low = (table - high.astype(np.float64)).astype(jnp.bfloat16)
        return np.concatenate([high, low], axis=axis)

    return split(forward, 0), split(inverse, 1)


def pack_kernel(
    features_hbm, filter_hbm, taps_hbm, gain_hbm, out_hbm, weights_ref, query_ref,
    features_ref, filter_ref, taps_ref, gain_ref, extended, edges, rows, turned, packed, sems, out_sems,
):
    groups = out_hbm.shape[0]
    channels = LANES // groups
    streams = features_ref.shape[1]
    taps = taps_ref.shape[1]
    rim = taps - 1
    copies = [
        pltpu.make_async_copy(taps_hbm, taps_ref, sems.at[3]),
        pltpu.make_async_copy(features_hbm.at[0], features_ref.at[0], sems.at[0]),
        pltpu.make_async_copy(features_hbm.at[1], features_ref.at[1], sems.at[1]),
        pltpu.make_async_copy(filter_hbm, filter_ref, sems.at[2]),
        pltpu.make_async_copy(gain_hbm, gain_ref, sems.at[4]),
    ]
    for place in (3, 0, 1, 2, 4):
        copies[place].start()

    sent = []

    def put(row, tile):
        packed[row] = tile.T.astype(jnp.bfloat16).reshape(groups, channels, LANES)
        copy = pltpu.make_async_copy(packed.at[row], out_hbm.at[:, row], out_sems.at[row])
        copy.start()
        sent.append(copy)

    extended[:, :8] = jnp.zeros((streams, 8, LANES), jnp.float32)
    edges[...] = jnp.zeros_like(edges)
    rows[...] = jnp.zeros_like(rows)
    copies[3].wait()
    for half in range(2):
        put(2 + half, filter_ref[half].astype(jnp.float32))
    copies[0].wait()
    for half in range(2):
        copies[1 + half].wait()
        featured = []
        for stream in range(streams):
            value = features_ref[half, stream].astype(jnp.float32)
            extended[stream, 8:] = value
            base = 2 * rim * (half * streams + stream)
            edges[base : base + rim] = extended[stream, 8 + LANES - rim : 8 + LANES]
            edges[base + rim : base + 2 * rim] = extended[stream, 8 : 8 + rim]
            summed = taps_ref[stream, 0:1].astype(jnp.float32) * value
            for i in range(1, taps):
                weight = taps_ref[stream, i : i + 1].astype(jnp.float32)
                summed = summed + weight * extended[stream, 8 - i : 8 - i + LANES]
            featured.append(summed)
        query_ref[half] = featured[0]
        put(half, featured[1] * featured[2])
    put(4, edges[...])
    copies[4].wait()
    for stream in range(streams):
        rows[stream * 8 : stream * 8 + taps] = taps_ref[stream].astype(jnp.float32)
    rows[streams * 8 : streams * 8 + 1] = gain_ref[...]
    turned[...] = rows[...].T
    position = (lax.axis_index("ctx") + groups - CTX_FIRST) % groups
    first = pl.multiple_of(position * channels, channels)
    weights_ref[...] = turned[pl.ds(first, channels)]
    for copy in sent:
        copy.wait()


def mix_kernel(
    packed_ref, weights_ref, forward_ref, inverse_ref, out_ref,
    query, keys, lags, key_spec, lag_spec, resp, total,
):
    pairs = packed_ref.shape[0]
    blocks = 2 * pairs
    channels = packed_ref.shape[2]
    streams, taps = 3, 7
    rim = taps - 1
    step = 2 * rim
    lane = lax.broadcasted_iota(jnp.int32, (channels, LANES), 1)

    def place(block):
        owner, half = (block, 0) if block < pairs else (blocks - 1 - block, 1)
        return (owner - CTX_FIRST) % pairs, half

    def span(block):
        return slice(block * channels, (block + 1) * channels)

    def column(index):
        return jnp.broadcast_to(weights_ref[:, index : index + 1], (channels, LANES))

    for block in range(blocks):
        source, half = place(block)
        lags[span(block)] = packed_ref[source, 2 + half]
    stream_of = lane // step % streams
    weight = [
        jnp.where(stream_of == 0, column(i), jnp.where(stream_of == 1, column(8 + i), column(16 + i)))
        for i in range(taps)
    ]
    tail = lane % step < rim
    lower = lane < streams * step
    edge = [packed_ref[place(owner)[0], 4].astype(jnp.float32) for owner in range(pairs)]
    head = lane < rim
    for owner in range(pairs):
        before = edge[owner - 1] if owner else jnp.zeros_like(edge[0])
        if owner + 1 < pairs:
            after = edge[owner + 1]
        else:
            after = pltpu.roll(edge[owner], streams * step, 1)
        value = jnp.where(tail, jnp.where(lower, before, after), edge[owner])
        summed = weight[0] * value
        for i in range(1, taps):
            summed = summed + weight[i] * pltpu.roll(value, i, 1)
        product = summed * pltpu.roll(summed, LANES - step, 1)
        for half, block in ((0, owner), (1, blocks - 1 - owner)):
            first = half * streams * step + rim
            gated = pltpu.roll(product, LANES - first - step, 1)
            whole = packed_ref[place(owner)[0], half].astype(jnp.float32)
            keys[span(block)] = jnp.where(head, gated, whole).astype(jnp.bfloat16)
            query[span(block)] = pltpu.roll(summed, LANES - first, 1)

    def transform(values):
        return jnp.dot(
            jnp.concatenate([values, values], axis=1), forward_ref[...], preferred_element_type=jnp.float32
        )

    key_spec[...] = transform(keys[...])
    lag_spec[...] = transform(lags[...])
    parity = jnp.where(lane % 2 == 0, 1.0, -1.0).astype(jnp.float32)
    for block in range(blocks):
        real = lag_spec[span(block), :LANES]
        imag = lag_spec[span(block), LANES:]
        if block:
            real = real + parity * lag_spec[span(block - 1), :LANES]
            imag = imag + parity * lag_spec[span(block - 1), LANES:]
        cross = jnp.where(lane == 0, 0.0, imag)
        resp[0, span(block)] = real + cross
        resp[1, span(block)] = cross
        resp[2, span(block)] = jnp.where(lane == 0, imag, real) - cross
    group = 4
    for base in range(0, blocks, group):
        sums = [None] * group
        held = {}
        for block in range(base + group):
            real = key_spec[span(block), :LANES]
            imag = key_spec[span(block), LANES:]
            both = real + imag
            for j in range(group):
                gap = base + j - block
                if gap < 0:
                    continue
                if gap not in held:
                    held[gap] = [resp[i, span(gap)] for i in range(3)]
                terms = [one * other for one, other in zip((real, both, imag), held[gap])]
                if sums[j] is not None:
                    terms = [one + other for one, other in zip(sums[j], terms)]
                sums[j] = terms
        for j in range(group):
            total[span(base + j), :LANES] = sums[j][0] - sums[j][1]
            total[span(base + j), LANES:] = sums[j][1] + sums[j][2]
    high = total[...].astype(jnp.bfloat16)
    low = (total[...] - high.astype(jnp.float32)).astype(jnp.bfloat16)
    wide = jnp.dot(high, inverse_ref[...], preferred_element_type=jnp.float32)
    narrow = jnp.dot(low, inverse_ref[:, :LANES], preferred_element_type=jnp.float32)
    total[:, :LANES] = wide[:, :LANES] + (wide[:, LANES:] + narrow)
    gain = column(24)
    for block in range(blocks):
        owner, half = (block, 0) if block < pairs else (blocks - 1 - block, 1)
        target = (owner - BACK_FIRST) % pairs
        inner = total[span(block), :LANES] + gain * keys[span(block)].astype(jnp.float32)
        out_ref[target, half] = jnp.where(head, query[span(block)] * inner, inner).astype(jnp.bfloat16)


def activate_kernel(mixed_ref, query_ref, out_ref):
    groups, halves, channels, length = mixed_ref.shape
    start = (CTX_FIRST - BACK_FIRST) % groups
    rim = 6
    token = lax.broadcasted_iota(jnp.int32, (length, LANES), 0)
    for half in range(halves):
        parts = [mixed_ref[start:, half], mixed_ref[:start, half]]
        inner = jnp.concatenate(parts, axis=0).reshape(groups * channels, length).astype(jnp.float32).T
        product = jnp.where(token < rim, inner, query_ref[half] * inner)
        out_ref[half * length : (half + 1) * length] = product.astype(jnp.bfloat16)


def regroup_kernel(
    own_hbm, other_hbm, forward_hbm, inverse_hbm, out_ref, forward_ref, inverse_ref, sems, table_sems
):
    chips = out_ref.shape[0] * out_ref.shape[2] // LANES
    step = chips // out_ref.shape[0]
    depth = own_hbm.shape[0]
    core = lax.axis_index("core")
    copies = [
        pltpu.make_async_copy(forward_hbm, forward_ref, table_sems.at[0]),
        pltpu.make_async_copy(inverse_hbm, inverse_ref, table_sems.at[1]),
    ]
    for chip in range(chips):
        block = 2 * ((chip + CHIP_FIRST) % chips) + core
        source = pl.ds(pl.multiple_of(block * LANES, LANES), LANES)
        columns = slice(chip % step * LANES, (chip % step + 1) * LANES)
        for i, weight in enumerate((own_hbm, other_hbm)):
            rows = pl.ds(pl.multiple_of((core + i) % 2 * depth, depth), depth)
            target = out_ref.at[chip // step, rows, columns]
            copies.append(pltpu.make_async_copy(weight.at[:, source], target, sems.at[i, chip]))
    for copy in copies:
        copy.start()
    for copy in copies:
        copy.wait()


def project_kernel(both_ref, weight_ref, out_ref):
    width = out_ref.shape[2]
    lhs = jnp.concatenate([both_ref[0], both_ref[1]], axis=1)
    step = weight_ref.shape[2] // width
    for group in range(weight_ref.shape[0]):
        product = jnp.dot(lhs, weight_ref[group], preferred_element_type=jnp.float32).astype(jnp.bfloat16)
        for i in range(step):
            out_ref[group * step + i] = product[:, i * width : (i + 1) * width]


def local(features, short_weight, long_filter, skip_gain, out_weight):
    pairs = lax.axis_size("ctx")
    chips = lax.axis_size("chip")
    length = features.shape[2]
    width = features.shape[4]
    channels = width // pairs
    order = [[(place + CTX_FIRST) % pairs for place in range(pairs)]]
    back_order = [[(place + BACK_FIRST) % pairs for place in range(pairs)]]
    chip_order = [[(place + CHIP_FIRST) % chips for place in range(chips)]]
    tiles = jnp.transpose(features, (0, 1, 3, 2, 4)).reshape(2, 3, length, width)
    taps = jnp.transpose(short_weight, (1, 0, 2))
    vmem = pl.BlockSpec(memory_space=pltpu.VMEM)
    hbm = pl.BlockSpec(memory_space=pltpu.HBM)
    packed, weights, query = pl.pallas_call(
        pack_kernel,
        out_shape=(
            pltpu.HBM((pairs, 5, channels, length), jnp.bfloat16),
            pltpu.VMEM((channels, LANES), jnp.float32),
            pltpu.VMEM((2, length, width), jnp.float32),
        ),
        in_specs=[hbm] * 4,
        out_specs=(hbm, vmem, vmem),
        scratch_shapes=[
            pltpu.VMEM((2, 3, length, width), jnp.bfloat16),
            pltpu.VMEM((2, length, width), jnp.bfloat16),
            pltpu.VMEM(taps.shape, jnp.bfloat16),
            pltpu.VMEM((1, width), jnp.float32),
            pltpu.VMEM((3, 8 + length, width), jnp.float32),
            pltpu.VMEM((LANES, LANES), jnp.float32),
            pltpu.VMEM((LANES, LANES), jnp.float32),
            pltpu.VMEM((LANES, LANES), jnp.float32),
            pltpu.VMEM((5, pairs, channels, length), jnp.bfloat16),
            pltpu.SemaphoreType.DMA((5,)),
            pltpu.SemaphoreType.DMA((5,)),
        ],
        compiler_params=pltpu.CompilerParams(vmem_limit_bytes=4 * MIB),
        cost_estimate=pl.CostEstimate(flops=1000000, bytes_accessed=600000, transcendentals=0),
        interpret=INTERPRET,
    )(
        in_hbm(tiles),
        in_hbm(long_filter.reshape(2, length, width)),
        in_hbm(taps),
        in_hbm(skip_gain.reshape(1, width)),
    )
    packed = lax.all_to_all(packed, "ctx", 0, 0, tiled=True, axis_index_groups=order)
    other_weight = lax.ppermute(out_weight, "core", [(0, 1), (1, 0)])
    step = math.gcd(chips, 2)
    forward, inverse = tables()
    columns, forward, inverse = pl.pallas_call(
        regroup_kernel,
        out_shape=(
            pltpu.VMEM((chips // step, 2 * width, step * width), jnp.bfloat16),
            pltpu.VMEM(forward.shape, jnp.bfloat16),
            pltpu.VMEM(inverse.shape, jnp.bfloat16),
        ),
        in_specs=[hbm, pl.BlockSpec(memory_space=pl.ANY), hbm, hbm],
        out_specs=(vmem, vmem, vmem),
        scratch_shapes=[pltpu.SemaphoreType.DMA((2, chips)), pltpu.SemaphoreType.DMA((2,))],
        compiler_params=pltpu.CompilerParams(vmem_limit_bytes=4 * MIB),
        cost_estimate=pl.CostEstimate(flops=0, bytes_accessed=2 * MIB, transcendentals=0),
        interpret=INTERPRET,
    )(
        in_hbm(out_weight),
        other_weight,
        in_hbm(jnp.asarray(forward)),
        in_hbm(jnp.asarray(inverse)),
    )
    rows = 2 * pairs * channels
    mixed = pl.pallas_call(
        mix_kernel,
        out_shape=pltpu.VMEM((pairs, 2, channels, length), jnp.bfloat16),
        in_specs=[vmem] * 4,
        out_specs=vmem,
        scratch_shapes=[
            pltpu.VMEM((rows, LANES), jnp.float32),
            pltpu.VMEM((rows, LANES), jnp.bfloat16),
            pltpu.VMEM((rows, LANES), jnp.bfloat16),
            pltpu.VMEM((rows, PERIOD), jnp.float32),
            pltpu.VMEM((rows, PERIOD), jnp.float32),
            pltpu.VMEM((3, rows, LANES), jnp.float32),
            pltpu.VMEM((rows, PERIOD), jnp.float32),
        ],
        compiler_params=pltpu.CompilerParams(vmem_limit_bytes=6 * MIB),
        cost_estimate=pl.CostEstimate(flops=100000000, bytes_accessed=600000, transcendentals=0),
        interpret=INTERPRET,
    )(
        packed,
        weights,
        forward,
        inverse,
    )
    mixed = lax.all_to_all(mixed, "ctx", 0, 0, tiled=True, axis_index_groups=back_order)
    activated = pl.pallas_call(
        activate_kernel,
        out_shape=pltpu.VMEM((2 * length, width), jnp.bfloat16),
        in_specs=[vmem] * 2,
        out_specs=vmem,
        compiler_params=pltpu.CompilerParams(vmem_limit_bytes=4 * MIB),
        cost_estimate=pl.CostEstimate(flops=1000000, bytes_accessed=300000, transcendentals=0),
        interpret=INTERPRET,
    )(mixed, query)
    both = lax.all_gather(activated, "core", axis=0)
    partial = pl.pallas_call(
        project_kernel,
        out_shape=pltpu.VMEM((chips, 2 * length, width), jnp.bfloat16),
        in_specs=[vmem] * 2,
        out_specs=vmem,
        compiler_params=pltpu.CompilerParams(vmem_limit_bytes=8 * MIB),
        cost_estimate=pl.CostEstimate(flops=268435456, bytes_accessed=3300000, transcendentals=0),
        interpret=INTERPRET,
    )(both, columns)
    shares = lax.all_to_all(partial, "chip", 0, 0, tiled=True, axis_index_groups=chip_order)
    result = jnp.sum(shares.astype(jnp.float32), axis=0).astype(jnp.bfloat16)
    return result.reshape(2, 1, length, width)


def solution(mesh):
    pairs, parts = mesh.shape["ctx"], mesh.shape["ch"]
    split = Mesh(mesh.devices.reshape(pairs, parts // 2, 2), ("ctx", "chip", "core"))
    ch = ("chip", "core")
    in_specs = (
        P(None, "ctx", None, None, ch),
        P(None, None, ch),
        P(None, "ctx", None, ch),
        P(ch),
        P(ch, None),
    )
    return jax.shard_map(local, mesh=split, in_specs=in_specs, out_specs=P(None, "ctx", None, ch), check_vma=False)
```
